32 devices in a mesh: groups: 2 (over y), patch: 8 (over z, x), visit: 2 (over core).
Axes of the slice: x: 2, y: 2, z: 4, core: 2. Of those that a mesh axis runs over, the one named last changes fastest.
Arguments:
- visit_tiles: bfloat16 [1792, 64, 1024], P(('groups', 'patch', 'visit')), parts along dimension 0, may hold values from -6 to 6
- tile_patch: int32 [1792], P(('groups', 'patch', 'visit')), parts along dimension 0, may hold values from 0 to 7, as said below
- offsets: int32 [1792, 2], P(('groups', 'patch', 'visit')), parts along dimension 0, may hold values from -128 to 127
- psf_coefs: int32 [1792, 3], P(('groups', 'patch', 'visit')), parts along dimension 0, may hold values from 16 to 80
- weights: bfloat16 [1792], P(('groups', 'patch', 'visit')), parts along dimension 0, may hold values from 0.19921875 to 4
Outputs:
- coadd: float32 [1024, 1024], P(('groups', 'patch')), parts along dimension 0
- detection: float32 [1024, 1024], P(('groups', 'patch')), parts along dimension 0
The draws below stay inside these ranges and needn't reach their ends.
There are 2 independent parts, one for each index of `groups`. The reference program is written for one: setup_inputs(seed, part) draws one part's arguments, and reference() takes and returns one part's arrays. A program takes and returns all parts, laid end to end along the dimension named above; each array names one. Nothing has to cross between parts.
Inputs may be any that keep to these rules, and one draw needn't show every extreme that they name: `tile_patch`: among the 56 tiles of one device at most 14 name any one patch; 2 deep-field patches are named by exactly 14 tiles of every device; every patch is named by some tile.
All inputs are finite; a program needn't handle non-finite values.
Results may differ from the reference program's by a relative error of at most 0.0048.
Values may be sent and summed in bfloat16 or wider, within the bound.
No kernel may reach another device: no remote copies, remote signals or barrier semaphores. Data moves between devices by JAX's collectives and lax.ppermute only.
A program may use at most 128 MiB of HBM per device.

```python
import math
import jax
import jax.numpy as jnp
from jax import lax

PH = 64
PW = 1024
TILES_DEV = 56
HALO = 8
DEEP = 2
PATCHES = 8
CAP = 14
TILES = 896


def draw_tile_patch(key, part):
    block_count = TILES // TILES_DEV
    slot_total = PATCHES * CAP
    deep_patches = jax.random.permutation(jax.random.fold_in(key, 7), PATCHES)[:DEEP].astype(jnp.int32)
    slot_patch = jnp.arange(slot_total, dtype=jnp.int32) // CAP
    slot_within = jnp.arange(slot_total, dtype=jnp.int32) % CAP
    is_deep = jnp.any(slot_patch[:, None] == deep_patches[None, :], axis=1)

    def one_block(block_key, block_index):
        first_key, second_key = jax.random.split(block_key)
        order_rank = jax.random.permutation(first_key, slot_total).astype(jnp.int32)
        covered = (slot_patch == block_index % PATCHES) & (slot_within == 0)
        priority = jnp.where(is_deep | covered, -1, order_rank)
        chosen = jnp.argsort(priority, stable=True)[:TILES_DEV]
        picked = slot_patch[chosen]
        return picked[jax.random.permutation(second_key, TILES_DEV)]
    block_keys = jax.random.split(jax.random.fold_in(key, 11), block_count)
    block_ids = jnp.arange(block_count, dtype=jnp.int32)
    return jax.vmap(one_block)(block_keys, block_ids).reshape(-1).astype(jnp.int32)


def set_ends(drawn, own_key, least, top_value):
    spot = [jax.random.randint(jax.random.fold_in(own_key, axis), (), 0, length) for axis, length in enumerate(drawn.shape)]
    main_axis = drawn.shape.index(max(drawn.shape))
    neighbour = spot[:main_axis] + [(spot[main_axis] + 1) % drawn.shape[main_axis]] + spot[main_axis + 1:]
    return drawn.at[tuple(spot)].set(least).at[tuple(neighbour)].set(top_value)


def shard_levels(rng, shape, pieces, smallest, high):
    factor_of = 1.0
    for dim, parts in pieces:
        draws = jax.random.uniform(jax.random.fold_in(jax.random.fold_in(rng, 6), dim), (parts,), jnp.float32, smallest / len(pieces), high / len(pieces))
        factor_of = factor_of * jnp.repeat(jnp.exp(draws), shape[dim] // parts).reshape((-1,) + (1,) * (len(shape) - 1 - dim))
    return factor_of


def bell_draw(stream_key, dims, scale, limit, cuts=(), kind=jnp.bfloat16):
    array = jax.random.normal(stream_key, dims, jnp.float32) * scale
    if len(cuts) > 0:
        array = shard_levels(stream_key, dims, cuts, -0.22, 0.18) * array
    return jnp.clip(array, min=-limit, max=limit).astype(kind)


def setup_inputs(seed: int = 0, part: int = 0) -> dict:
    splits = jax.random.split(jax.random.key(seed), 6)
    part_keys = jax.random.split(jax.random.fold_in(splits[5], part), 6)
    return {
        "visit_tiles": bell_draw(part_keys[0], (TILES, PH, PW), 1.0, 6.0, ((0, 16),)),
        "tile_patch": draw_tile_patch(jax.random.fold_in(jax.random.fold_in(splits[5], part), 71), part),
        "offsets": set_ends(jax.random.randint(part_keys[2], (TILES, 2), -128, 128), jax.random.fold_in(part_keys[2], 1), -128, 127).astype(jnp.int32),
        "psf_coefs": set_ends(jax.random.randint(part_keys[3], (TILES, 3), 16, 81), jax.random.fold_in(part_keys[3], 1), 16, 80).astype(jnp.int32),
        "weights": jnp.clip(jnp.exp(math.log(4.0) - 2.9996462 * jax.random.uniform(part_keys[4], (TILES,), jnp.float32) ** shard_levels(part_keys[4], (TILES,), ((0, 16),), -0.2, 0.2)), 0.19921875, 4.0).astype(jnp.bfloat16),
    }


PSF_SIGMAS = (0.75, 1.5, 3.0)
psf_reach = 16

def lanczos(value):
    inside = jnp.abs(value) < 3.0
    return jnp.where(inside, jnp.sinc(value) * jnp.sinc(value / 3.0), 0.0)

def gaussian(distance, sigma, reach):
    shape = jnp.exp(-distance * distance / (2.0 * sigma * sigma)) / (math.pi * sigma * sigma) ** 0.25
    return jnp.where(jnp.abs(distance) <= reach, shape, 0.0)

def shift_axis(image, offset, axis):
    whole_shift = offset // 64
    frac_shift = (offset - 64 * whole_shift).astype(jnp.float32) / 64.0
    length = image.shape[axis]
    widths = [(0, 0), (0, 0)]
    widths[axis] = (5, 5)
    padded = jnp.pad(image, widths)
    running = jnp.zeros(image.shape, jnp.float32)
    for tap_index in range(-2, 4):
        tap_weight = lanczos(frac_shift - tap_index).astype(jnp.bfloat16).astype(jnp.float32)
        start = (5 + whole_shift + tap_index).astype(jnp.int32)
        piece = lax.dynamic_slice_in_dim(padded, start, length, axis)
        running = running + tap_weight * piece.astype(jnp.float32)
    return running.astype(jnp.bfloat16)

def warp_ref(tile, offset):
    shifted = shift_axis(tile, offset[0], 0)
    return shift_axis(shifted, offset[1], 1)

def apply_taps(field, axis, sigma, reach):
    length = field.shape[axis]
    widths = [(0, 0)] * field.ndim
    widths[axis] = (reach, reach)
    padded = jnp.pad(field, widths)
    running = jnp.zeros(field.shape, jnp.float32)
    for distance in range(-reach, reach + 1):
        coeff = gaussian(jnp.float32(distance), sigma, reach)
        piece = lax.slice_in_dim(padded, reach - distance, reach - distance + length, axis=axis)
        running = running + coeff * piece
    return running

def reference(visit_tiles, tile_patch, offsets, psf_coefs, weights):
    block_count = TILES // TILES_DEV
    blocks = (visit_tiles.reshape(block_count, TILES_DEV, PH, PW), tile_patch.reshape(block_count, TILES_DEV), offsets.reshape(block_count, TILES_DEV, 2), psf_coefs.reshape(block_count, TILES_DEV, 3), weights.reshape(block_count, TILES_DEV))

    def accumulate(carry, block):
        stacks, weight_sq = carry
        tiles_blk, patch_blk, offset_blk, coef_blk, weight_blk = block
        warped = jax.vmap(warp_ref)(tiles_blk, offset_blk)
        weight_f = weight_blk.astype(jnp.float32)
        factor = weight_f[:, None] * (coef_blk.astype(jnp.float32) / 64.0)
        contrib = factor[:, :, None, None] * warped.astype(jnp.float32)[:, None]
        stacks = stacks.at[patch_blk].add(contrib)
        weight_sq = weight_sq.at[patch_blk].add(weight_f * weight_f)
        return ((stacks, weight_sq), None)
    start = (jnp.zeros((PATCHES, 3, PH, PW), jnp.float32), jnp.zeros((PATCHES,), jnp.float32))
    (stacks, weight_sq), _ = lax.scan(accumulate, start, blocks)
    matched = jnp.zeros((PATCHES, PH, PW), jnp.float32)
    for basis in range(3):
        sigma = PSF_SIGMAS[basis]
        blurred = apply_taps(stacks[:, basis], 1, sigma, psf_reach)
        matched = matched + apply_taps(blurred, 2, sigma, psf_reach)
    coadd = (matched / jnp.sqrt(weight_sq)[:, None, None]).reshape(PATCHES * PH, PW)
    detect_sigma = HALO / 4.0
    detection = apply_taps(apply_taps(coadd, 0, detect_sigma, HALO), 1, detect_sigma, HALO)
    return (coadd, detection)
```

```python
import functools
import math

import jax
import jax.numpy as jnp
import numpy as np
from jax import lax
from jax.experimental import pallas as pl
from jax.experimental.pallas import tpu as pltpu
from jax.sharding import PartitionSpec as P

BF16, F32, I32 = jnp.bfloat16, jnp.float32, jnp.int32
HALO = 8
PSF_SIGMAS = (0.75, 1.5, 3.0)
PSF_REACH = 16
BASES = len(PSF_SIGMAS)
LANES = 128
GROUP = 4


def gaussian(distance, sigma, reach):
    shape = np.exp(-distance * distance / (2.0 * sigma * sigma)) / (math.pi * sigma * sigma) ** 0.25
    return np.where(np.abs(distance) <= reach, shape, 0.0)


def split_bf16(value):
    high = value.astype(BF16)
    return high, (value - high.astype(F32)).astype(BF16)


def row_filters(rows):
    index = np.arange(rows, dtype=np.float64)
    offset = index[:, None] - index[None, :]
    stacked = np.concatenate([gaussian(offset, s, PSF_REACH) for s in PSF_SIGMAS], axis=0)
    high = stacked.astype(np.float32).astype(BF16)
    low = (stacked.astype(np.float32) - high.astype(np.float32)).astype(BF16)
    return np.concatenate([high, low], axis=1)


def col_filter(sigma, reach):
    lane = np.arange(LANES, dtype=np.float64)
    offset = lane[None, :] - lane[:, None]
    wrapped = (offset + LANES // 2) % LANES - LANES // 2
    circulant = gaussian(wrapped, sigma, reach)
    own = np.where(np.abs(offset) < LANES // 2, circulant, 0.0)
    edge = np.where(np.abs(offset) >= LANES // 2, circulant, 0.0)
    return np.concatenate([own, edge], axis=0)


def windows(blocks):
    rows = blocks[0].shape[0]
    left = lax.broadcasted_iota(I32, (rows, LANES), 1) < LANES // 2
    zero = jnp.zeros_like(blocks[0])
    padded = [zero, *blocks, zero]
    return jnp.concatenate(
        [
            jnp.concatenate([padded[b + 1], jnp.where(left, padded[b + 2], padded[b])], axis=1)
            for b in range(len(blocks))
        ],
        axis=0,
    )


def lanczos(value):
    angle = math.pi * jnp.where(jnp.abs(value) < 3.0, value, 1.0)
    safe = jnp.where(angle == 0.0, 1.0, angle)
    shape = jnp.sin(safe) * jnp.sin(safe / 3.0) * (3.0 / (safe * safe))
    inside = jnp.where(angle == 0.0, 1.0, shape)
    return jnp.where(jnp.abs(value) < 3.0, inside, 0.0)


def stack_kernel(
    parity,
    patches,
    tile_patch,
    offsets,
    coefs,
    weights,
    tiles,
    row_mats,
    col_mats,
    out,
    out_weight,
    raw,
    shifted,
    mixers,
    total,
    row_taps,
    col_taps,
    sems,
    order,
    slot_key,
    first,
    cursor,
):
    me = lax.axis_index("patch")
    count, rows, cols = raw.shape
    keys = patches // 2
    blocks = cols // LANES

    def fetch(t):
        return pltpu.make_async_copy(tiles.at[t], raw.at[t], sems.at[t])

    def key_of(t):
        mixed = tile_patch[t] ^ me
        return jnp.where((mixed & 1) == parity, mixed >> 1, keys)

    for k in range(keys + 1):
        cursor[k] = 0

    def count_one(t, carry):
        key = key_of(t)
        cursor[key] += 1

        @pl.when(key < keys)
        def _():
            fetch(t).start()

        return carry

    lax.fori_loop(0, count, count_one, 0)
    running = 0
    for k in range(keys + 1):
        number = cursor[k]
        first[k] = running
        cursor[k] = running
        running = running + number
    live = first[keys]

    for k in range(keys):
        out_weight[k] = 0.0

    def place_one(t, carry):
        key = key_of(t)
        slot = cursor[key]
        cursor[key] = slot + 1
        order[slot] = t
        slot_key[slot] = key
        row_taps[pl.ds(t, 1), :] = jnp.full((1, LANES), offsets[0, t], I32).astype(F32) / 64.0
        col_taps[pl.ds(t, 1), :] = jnp.full((1, LANES), offsets[1, t], I32).astype(F32) / 64.0

        @pl.when(key < keys)
        def _():
            out_weight[key] += weights[t] * weights[t]

        return carry

    lax.fori_loop(0, count, place_one, 0)

    lane = lax.broadcasted_iota(I32, (count, LANES), 1)
    wrapped = (((lane + LANES // 2) & (LANES - 1)) - LANES // 2).astype(F32)
    row_taps[...] = lanczos(row_taps[...] - wrapped)
    col_taps[...] = lanczos(col_taps[...] + wrapped)

    square = lax.broadcasted_iota(I32, (LANES, LANES), 1) - lax.broadcasted_iota(I32, (LANES, LANES), 0)
    inner = jnp.abs(square) < LANES // 2
    half = lax.broadcasted_iota(I32, (rows, LANES), 1) < LANES // 2
    half_row = lax.broadcasted_iota(I32, (1, LANES), 1) < LANES // 2

    def band(line, height):
        spread = jnp.broadcast_to(line, (height, LANES))
        return pltpu.roll(spread, 0, 1, stride=1, stride_axis=0)

    def warp_group(g, carry):
        ids, scales = [], []
        for j in range(GROUP):
            slot = g * GROUP + j
            t = order[jnp.minimum(slot, live - 1)]

            @pl.when(slot < live)
            def _():
                fetch(t).wait()

            ids.append(t)
            scales.append([weights[t] * (coefs[k, t].astype(F32) / 64.0) for k in range(BASES)])
        for j, t in enumerate(ids):
            circulant = band(col_taps[pl.ds(t, 1), :], LANES)
            spread = jnp.concatenate(
                [jnp.where(inner, circulant, 0.0), jnp.where(inner, 0.0, circulant)], axis=0
            ).astype(BF16)
            data = raw[t]
            window = windows([data[:, b * LANES : (b + 1) * LANES] for b in range(blocks)])
            moved = jnp.dot(window, spread, preferred_element_type=F32).astype(BF16)
            for b in range(blocks):
                shifted[g, j * rows : (j + 1) * rows, b * LANES : (b + 1) * LANES] = moved[
                    b * rows : (b + 1) * rows
                ]
        pairs = []
        for j in range(0, GROUP, 2):
            one = band(row_taps[pl.ds(ids[j], 1), :], rows)
            two = band(pltpu.roll(row_taps[pl.ds(ids[j + 1], 1), :], LANES // 2, 1), rows)
            pairs.append(jnp.where(half, one, two).astype(BF16))
        mixer = jnp.concatenate(pairs, axis=1)
        mixer = jnp.concatenate([mixer, mixer], axis=0)
        mixer = jnp.dot(row_mats[...], mixer, preferred_element_type=F32)
        for k in range(BASES):
            scale = jnp.concatenate(
                [
                    jnp.where(half_row, scales[j][k], scales[j + 1][k])
                    for j in range(0, GROUP, 2)
                ],
                axis=1,
            )
            mixers[g, k * rows : (k + 1) * rows, :] = (mixer[k * rows : (k + 1) * rows] * scale).astype(BF16)
        return carry

    lax.fori_loop(0, pl.cdiv(live, GROUP), warp_group, 0)

    which = lax.broadcasted_iota(I32, (1, GROUP * rows), 1) // rows

    def finish(k, carry):
        begin, end = first[k], first[k + 1]
        total[...] = jnp.zeros_like(total)

        def add_group(g, inner_carry):
            slots = which + g * GROUP
            mine = (slots >= begin) & (slots < end)
            mixer = jnp.where(mine, mixers[g], jnp.zeros((), BF16))
            total[...] += jnp.dot(mixer, shifted[g], preferred_element_type=F32)
            return inner_carry

        lax.fori_loop(begin // GROUP, pl.cdiv(end, GROUP), add_group, 0)
        stacked = []
        for k3 in range(BASES):
            base = total[k3 * rows : (k3 + 1) * rows, :].astype(BF16)
            stacked.append(windows([base[:, b * LANES : (b + 1) * LANES] for b in range(blocks)]))
        matched = jnp.dot(
            jnp.concatenate(stacked, axis=1), col_mats[...], preferred_element_type=F32
        )
        for b in range(blocks):
            out[k, :, b * LANES : (b + 1) * LANES] = matched[b * rows : (b + 1) * rows].astype(out.dtype)
        return carry

    lax.fori_loop(0, keys, finish, 0)


def local_stacks(parity, patches, tile_patch, offsets, coefs, weights, tiles, row_mats, col_mats):
    count, rows, cols = tiles.shape
    keys = patches // 2
    groups = -(-count // GROUP)
    smem = pl.BlockSpec(memory_space=pltpu.SMEM)
    vmem = pl.BlockSpec(memory_space=pltpu.VMEM)
    return pl.pallas_call(
        functools.partial(stack_kernel, parity, patches),
        out_shape=(
            jax.ShapeDtypeStruct((keys, rows, cols), F32),
            jax.ShapeDtypeStruct((keys,), F32),
        ),
        in_specs=[smem, smem, smem, smem, pl.BlockSpec(memory_space=pl.ANY), vmem, vmem],
        out_specs=(vmem, smem),
        scratch_shapes=[
            pltpu.VMEM((count, rows, cols), BF16),
            pltpu.VMEM((groups, GROUP * rows, cols), BF16),
            pltpu.VMEM((groups, BASES * rows, GROUP * rows), BF16),
            pltpu.VMEM((BASES * rows, cols), F32),
            pltpu.VMEM((count, LANES), F32),
            pltpu.VMEM((count, LANES), F32),
            pltpu.SemaphoreType.DMA((count,)),
            pltpu.SMEM((count,), I32),
            pltpu.SMEM((count,), I32),
            pltpu.SMEM((keys + 1,), I32),
            pltpu.SMEM((keys + 1,), I32),
        ],
        cost_estimate=pl.CostEstimate(
            flops=2 * count * rows * cols * 512, bytes_accessed=count * rows * cols, transcendentals=0
        ),
        name=f"stacks{parity}",
    )(tile_patch, offsets, coefs, weights, tiles, row_mats, col_mats)


def smooth_kernel(rows_mat, cols_mat, image, out):
    blocks = image.shape[1] // LANES
    rows = out.shape[0]
    high, low = split_bf16(image[...])
    row_high, row_low = rows_mat[0], rows_mat[1]
    blurred = (
        jnp.dot(row_high, high, preferred_element_type=F32)
        + jnp.dot(row_high, low, preferred_element_type=F32)
        + jnp.dot(row_low, high, preferred_element_type=F32)
    )
    high, low = split_bf16(blurred)
    parts = [
        windows([part[:, b * LANES : (b + 1) * LANES] for b in range(blocks)]) for part in (high, low)
    ]
    col_high, col_low = cols_mat[0], cols_mat[1]
    result = (
        jnp.dot(parts[0], col_high, preferred_element_type=F32)
        + jnp.dot(parts[1], col_high, preferred_element_type=F32)
        + jnp.dot(parts[0], col_low, preferred_element_type=F32)
    )
    for b in range(blocks):
        out[:, b * LANES : (b + 1) * LANES] = result[b * rows : (b + 1) * rows]


def smooth(extended, rows):
    sigma = HALO / 4.0
    out_index = np.arange(rows, dtype=np.float64)[:, None]
    in_index = np.arange(rows + 2 * HALO, dtype=np.float64)[None, :]

    def both(matrix):
        high = matrix.astype(np.float32).astype(BF16)
        low = (matrix.astype(np.float32) - high.astype(np.float32)).astype(BF16)
        return jnp.asarray(np.stack([high, low]))

    return pl.pallas_call(
        smooth_kernel,
        out_shape=jax.ShapeDtypeStruct((rows, extended.shape[1]), F32),
        name="smooth",
    )(both(gaussian(out_index + HALO - in_index, sigma, HALO)), both(col_filter(sigma, HALO)), extended)


def shards(visit_tiles, tile_patch, offsets, psf_coefs, weights):
    rows, cols = visit_tiles.shape[1:]
    owners = lax.axis_size("patch")
    keys = owners // 2
    row_mats = jnp.asarray(row_filters(rows))
    col_mats = jnp.asarray(
        np.concatenate([col_filter(s, PSF_REACH) for s in PSF_SIGMAS]).astype(np.float32).astype(BF16)
    )
    stacks = functools.partial(
        local_stacks,
        patches=owners,
        tile_patch=tile_patch,
        offsets=offsets.T,
        coefs=psf_coefs.T,
        weights=weights.astype(F32),
        tiles=visit_tiles,
        row_mats=row_mats,
        col_mats=col_mats,
    )
    helper = lax.axis_index("visit")
    half = rows // 2

    def over_visit(part, weight):
        mine = lax.dynamic_slice_in_dim(part, helper * half, half, axis=1)
        other = lax.dynamic_slice_in_dim(part, (1 - helper) * half, half, axis=1)
        swap = [(0, 1), (1, 0)]
        return (
            mine + lax.ppermute(other.astype(BF16), "visit", swap).astype(F32),
            weight + lax.ppermute(weight, "visit", swap),
        )

    far, far_weight = over_visit(*stacks(1))
    beside = [(i, i ^ 1) for i in range(owners)]
    got = lax.ppermute(far.astype(BF16), "patch", beside)
    got_weight = lax.ppermute(far_weight, "patch", beside)
    near, near_weight = over_visit(*stacks(0))
    near = near + got.astype(F32)
    near_weight = near_weight + got_weight
    sent = near.astype(BF16)
    total, weight = near[0], near_weight[0]
    for d in range(1, keys):
        hop = [(i, i ^ (2 * d)) for i in range(owners)]
        total = total + lax.ppermute(sent[d], "patch", hop).astype(F32)
        weight = weight + lax.ppermute(near_weight[d], "patch", hop)
    mine = total / jnp.sqrt(weight)
    other = lax.ppermute(mine, "visit", [(0, 1), (1, 0)])
    upper = jnp.where(helper == 0, mine, other)
    lower = jnp.where(helper == 0, other, mine)
    coadd = jnp.concatenate([upper, lower], axis=0)
    up = [(i, i + 1) for i in range(owners - 1)]
    down = [(j, i) for i, j in up]
    before = lax.ppermute(coadd[-HALO:].astype(BF16), "patch", up).astype(F32)
    after = lax.ppermute(coadd[:HALO].astype(BF16), "patch", down).astype(F32)
    extended = jnp.concatenate([before, coadd, after], axis=0)
    return coadd, smooth(extended, rows)


def solution(mesh):
    placed = (
        P(("groups", "patch", "visit"), None, None),
        P(("groups", "patch", "visit")),
        P(("groups", "patch", "visit"), None),
        P(("groups", "patch", "visit"), None),
        P(("groups", "patch", "visit")),
    )
    return jax.shard_map(
        shards,
        mesh=mesh,
        in_specs=placed,
        out_specs=(P(("groups", "patch"), None), P(("groups", "patch"), None)),
        check_vma=False,
    )
```

```python
import functools
import math

import jax
import jax.numpy as jnp
import numpy as np
from jax import lax
from jax.experimental import pallas as pl
from jax.experimental.pallas import tpu as pltpu
from jax.sharding import PartitionSpec as P


BF16, F32, I32 = jnp.bfloat16, jnp.float32, jnp.int32
HALO = 8
PSF_SIGMAS = (0.75, 1.5, 3.0)
PSF_REACH = 16
BASES = len(PSF_SIGMAS)
LANES = 128
WIDE = 2 * LANES
GROUP = 4
STEPS = 64
OFFSET_MAX = 128
WEIGHT_BITS = 10
WARP_SEGMENT, WARP_EDGE = 32, 8
PSF_SEGMENT, PSF_EDGE = 64, 16


def gaussian(distance, sigma, reach):
    shape = np.exp(-distance * distance / (2.0 * sigma * sigma)) / (math.pi * sigma * sigma) ** 0.25
    return np.where(np.abs(distance) <= reach, shape, 0.0)


def to_bf16(value):
    return value.astype(np.float32).astype(BF16)


def row_filters(rows):
    index = np.arange(rows, dtype=np.float64)
    offset = index[:, None] - index[None, :]
    stacked = np.concatenate([gaussian(offset, s, PSF_REACH) for s in PSF_SIGMAS], axis=0)
    high = to_bf16(stacked)
    return np.concatenate([high, to_bf16(stacked - high.astype(np.float64))], axis=1)


def psf_col_filters():
    lane = np.arange(WIDE, dtype=np.float64)
    offset = lane[None, :] - lane[:, None]
    same = (lane[None, :] // PSF_SEGMENT) == (lane[:, None] // PSF_SEGMENT)
    bands = [gaussian(offset, s, PSF_REACH) for s in PSF_SIGMAS]
    main = np.concatenate(bands, axis=0)
    edge = np.concatenate([np.where(same, band, 0.0) for band in bands], axis=0)
    return to_bf16(main), to_bf16(edge)


def col_filter(sigma, reach):
    lane = np.arange(LANES, dtype=np.float64)
    offset = lane[None, :] - lane[:, None]
    wrapped = (offset + LANES // 2) % LANES - LANES // 2
    circulant = gaussian(wrapped, sigma, reach)
    own = np.where(np.abs(offset) < LANES // 2, circulant, 0.0)
    edge = np.where(np.abs(offset) >= LANES // 2, circulant, 0.0)
    return to_bf16(np.concatenate([own, edge], axis=0))


def lanczos_lines():
    lane = np.arange(LANES, dtype=np.float64)
    wrapped = (lane + LANES // 2) % LANES - LANES // 2
    offset = np.arange(-OFFSET_MAX, OFFSET_MAX + 8, dtype=np.float64)[:, None] / STEPS
    value = wrapped[None, :] + offset
    line = np.where(np.abs(value) < 3.0, np.sinc(value) * np.sinc(value / 3.0), 0.0)
    return line.astype(np.float32)


def digit_bits(devices):
    return max(1, int(math.log2(256 // devices)) if devices <= 128 else 1)


def power_of_two(exponent):
    out = 1.0
    for i in range(6):
        out = out * jnp.where((exponent >> i) & 1 == 1, 2.0 ** (2**i), 1.0)
    return out


def windows(blocks):
    rows = blocks[0].shape[0]
    left = lax.broadcasted_iota(I32, (rows, LANES), 1) < LANES // 2
    zero = jnp.zeros_like(blocks[0])
    padded = [zero, *blocks, zero]
    return jnp.concatenate(
        [
            jnp.concatenate([padded[b + 1], jnp.where(left, padded[b + 2], padded[b])], axis=1)
            for b in range(len(blocks))
        ],
        axis=0,
    )


def block(value, b):
    return value[:, b * LANES : (b + 1) * LANES]


def border_columns(value, segment):
    rows, cols = value.shape
    lane = lax.broadcasted_iota(I32, (rows, LANES), 1)
    per = LANES // segment
    borders = cols // WIDE - 1
    out = []
    for start in range(0, borders, per):
        merged = None
        for s in range(start, min(start + per, borders)):
            both = jnp.where(lane < LANES // 2, block(value, 2 * s + 2), block(value, 2 * s + 1))
            moved = pltpu.roll(both, segment // 2 + segment * (s - start), 1)
            merged = moved if merged is None else jnp.where(lane >= segment * (s - start), moved, merged)
        out.append(merged)
    return out


def mend_borders(blocks, edges, segment, reach):
    rows = blocks[0].shape[0]
    lane = lax.broadcasted_iota(I32, (rows, LANES), 1)
    per = LANES // segment
    blocks = list(blocks)
    for s in range(len(blocks) // 2 - 1):
        shift = LANES - segment // 2 - segment * (s % per)
        moved = pltpu.roll(edges[s // per], shift, 1)
        blocks[2 * s + 1] = jnp.where(lane >= LANES - reach, moved, blocks[2 * s + 1])
        blocks[2 * s + 2] = jnp.where(lane < reach, moved, blocks[2 * s + 2])
    return blocks


def side_by_side(value):
    return jnp.concatenate(
        [value[:, s : s + WIDE] for s in range(0, value.shape[1], WIDE)], axis=0
    )


def stack_kernel(stage, patches, bits, *refs):
    if stage == 0:
        tile_patch_in, raw_weights_in, offsets_in, coefs_in, tiles, *mats_in = refs[:9]
        send, keep, order, slot_key, first, weights, weight_sq = refs[9:16]
        refs = refs[16:]
    else:
        order, slot_key, first, weights, weight_sq, offsets_in, coefs_in, tiles, *mats_in = refs[:12]
        send, keep = refs[12:14]
        refs = refs[14:]
    raw, shifted, mixers, total, sems, offsets, coefs, lines, row_mats, col_main, col_edge, in_sems = refs[:12]
    moves = [
        pltpu.make_async_copy(source, target, in_sems.at[i])
        for i, (source, target) in enumerate(
            zip((offsets_in, coefs_in, *mats_in), (offsets, coefs, lines, row_mats, col_main, col_edge), strict=True)
        )
    ]
    if stage == 0:
        tile_patch, raw_weights, cursor, weight_line, weight_sem, first_sems = refs[12:]
        patch_move = pltpu.make_async_copy(tile_patch_in, tile_patch, first_sems.at[0])
        weight_move = pltpu.make_async_copy(raw_weights_in, raw_weights, first_sems.at[1])
        patch_move.start()
        weight_move.start()
    for move in moves:
        move.start()
    me = lax.axis_index("patch")
    helper = lax.axis_index("visit")
    count, rows, cols = tiles.shape
    keys = patches // 2
    half = rows // 2

    if stage == 0:
        weight_move.wait()
        weight_line[...] = raw_weights[...].astype(F32)
        weight_copy = pltpu.make_async_copy(weight_line, weights, weight_sem)
        weight_copy.start()

        def key_of(t):
            mixed = tile_patch[t] ^ me
            return ((mixed & 1) ^ 1) * keys + (mixed >> 1)

        patch_move.wait()
        for k in range(patches):
            cursor[k] = 0
        for t in range(count):
            cursor[key_of(t)] += 1
        running = 0
        for k in range(patches):
            number = cursor[k]
            first[k] = running
            cursor[k] = running
            weight_sq[k] = 0.0
            running = running + number
        first[patches] = running
        for t in range(count):
            key = key_of(t)
            slot = cursor[key]
            cursor[key] = slot + 1
            order[slot] = t
            slot_key[slot] = key

    low_key = stage * keys
    base = first[low_key]
    number = first[low_key + keys] - base
    groups = jnp.maximum(pl.cdiv(number, GROUP), 1)

    def tile_at(g, j):
        return order[jnp.clip(base + g * GROUP + j, 0, count - 1)]

    def key_at(g, j):
        slot = base + g * GROUP + j
        return jnp.where(slot < base + number, slot_key[jnp.clip(slot, 0, count - 1)], -1)

    def fetch(g, carry):
        for j in range(GROUP):
            pltpu.make_async_copy(tiles.at[tile_at(g, j)], raw.at[g, j], sems.at[g]).start()
        return carry

    lax.fori_loop(0, groups, fetch, 0)

    if stage == 0:
        weight_copy.wait()
        for t in range(count):
            key = key_of(t)
            weight_sq[key] += weights[t] * weights[t]

    square = lax.broadcasted_iota(I32, (LANES, LANES), 1) - lax.broadcasted_iota(I32, (LANES, LANES), 0)
    ahead, behind = square <= -LANES // 2, square >= LANES // 2
    inner = jnp.abs(square) < LANES // 2
    segment_of = lambda axis: lax.broadcasted_iota(I32, (LANES, LANES), axis) // WARP_SEGMENT
    same_segment = segment_of(0) == segment_of(1)
    half_lanes = lax.broadcasted_iota(I32, (rows, LANES), 1) < LANES // 2
    half_row = lax.broadcasted_iota(I32, (1, LANES), 1) < LANES // 2

    def band(line, height):
        spread = jnp.broadcast_to(line, (height, LANES))
        return pltpu.roll(spread, 0, 1, stride=1, stride_axis=0)

    def line_of(offset):
        return lines[pl.ds(jnp.clip(offset + OFFSET_MAX, 0, 2 * OFFSET_MAX), 1), :]

    def arrive(g):
        pltpu.make_async_copy(tiles.at[pl.ds(0, GROUP)], raw.at[g], sems.at[g]).wait()

    def warp(g):
        slot = g & 1
        ids = [tile_at(g, j) for j in range(GROUP)]
        for j in range(0, GROUP, 2):
            spreads, ends, end_mats = [], [], []
            for i in range(2):
                circulant = band(line_of(offsets[1, ids[j + i]]), LANES)
                pick = lambda mask: jnp.where(mask, circulant, 0.0).astype(BF16)
                own = pick(inner)
                spreads.append(
                    jnp.concatenate(
                        [
                            jnp.concatenate([own, pick(ahead)], axis=1),
                            jnp.concatenate([pick(behind), own], axis=1),
                        ],
                        axis=0,
                    )
                )
                ends.append(border_columns(raw[g, j + i], WARP_SEGMENT)[0])
                end_mats.append(pick(same_segment))
            empty = jnp.zeros((LANES, LANES), BF16)
            mats = jnp.concatenate(
                [
                    jnp.concatenate([end_mats[0], empty], axis=1),
                    jnp.concatenate([empty, end_mats[1]], axis=1),
                ],
                axis=0,
            )
            mended = jnp.dot(
                jnp.concatenate(ends, axis=1), mats, preferred_element_type=F32
            ).astype(BF16)
            for i in range(2):
                value = jnp.dot(
                    side_by_side(raw[g, j + i]), spreads[i], preferred_element_type=F32
                ).astype(BF16)
                blocks = [
                    block(value[s * rows : (s + 1) * rows], b) for s in range(cols // WIDE) for b in range(2)
                ]
                blocks = mend_borders(blocks, [block(mended, i)], WARP_SEGMENT, WARP_EDGE)
                for b, piece in enumerate(blocks):
                    shifted[slot, (j + i) * rows : (j + i + 1) * rows, b * LANES : (b + 1) * LANES] = piece
        pairs = []
        for j in range(0, GROUP, 2):
            one = band(line_of(-offsets[0, ids[j]]), rows)
            two = band(pltpu.roll(line_of(-offsets[0, ids[j + 1]]), LANES // 2, 1), rows)
            pairs.append(jnp.where(half_lanes, one, two).astype(BF16))
        mixer = jnp.concatenate(pairs, axis=1)
        mixer = jnp.concatenate([mixer, mixer], axis=0)
        mixer = jnp.dot(row_mats[...], mixer, preferred_element_type=F32)
        for k in range(BASES):
            scales = [weights[t] * (coefs[k, t].astype(F32) / STEPS) for t in ids]
            scale = jnp.concatenate(
                [jnp.where(half_row, scales[j], scales[j + 1]) for j in range(0, GROUP, 2)], axis=1
            )
            mixers[slot, k * rows : (k + 1) * rows, :] = (mixer[k * rows : (k + 1) * rows] * scale).astype(BF16)

    def group_sum(g, key):
        slot = g & 1
        owner = jnp.concatenate(
            [jnp.where(half_row, key_at(g, j), key_at(g, j + 1)) for j in range(0, GROUP, 2)], axis=1
        )
        mixer = jnp.where(owner == key, mixers[slot], jnp.zeros((), BF16))
        return jnp.dot(mixer, shifted[slot], preferred_element_type=F32)

    digit_row = lax.broadcasted_iota(I32, (half, LANES), 0)
    scale_up = power_of_two((digit_row + 1) * bits) * 2.0**-WEIGHT_BITS
    digit_live = digit_row * bits < WEIGHT_BITS + 30

    def finish(key, par):
        edges, mains = [], []
        for k in range(BASES):
            base_k = total[par, k * rows : (k + 1) * rows, :].astype(BF16)
            mains.append(side_by_side(base_k))
            edges.extend(border_columns(base_k, PSF_SEGMENT))
        main = jnp.dot(jnp.concatenate(mains, axis=1), col_main[...], preferred_element_type=F32)
        edge = jnp.dot(jnp.concatenate(edges, axis=1), col_edge[...], preferred_element_type=F32)
        blocks = [block(main[s * rows : (s + 1) * rows], b) for s in range(cols // WIDE) for b in range(2)]
        blocks = mend_borders(blocks, [block(edge, 0), block(edge, 1)], PSF_SEGMENT, PSF_EDGE)
        k = key - low_key
        upper = helper == 0
        for b, piece in enumerate(blocks):
            at = slice(b * LANES, (b + 1) * LANES)
            keep[k, :, at] = jnp.where(upper, piece[:half], piece[half:])
            send[k, :, at] = jnp.where(upper, piece[half:], piece[:half]).astype(BF16)
        scaled = jnp.floor(weight_sq[key] * jnp.where(digit_live, scale_up, 0.0))
        digits = scaled - 2.0**bits * jnp.floor(scaled * 2.0**-bits)
        keep[k, :, cols:] = digits
        send[k, :, cols:] = digits.astype(BF16)

    def close(g, key, par, key_end):
        def one(k, p):
            finish(k, p)
            total[1 - p] = group_sum(g, k + 1)
            return 1 - p

        return lax.fori_loop(key, key_end, one, par)

    total[0] = jnp.zeros(total.shape[1:], F32)
    for move in moves:
        move.wait()
    arrive(0)
    warp(0)

    def step(g, carry):
        key, par = carry
        arrive(g)
        total[par] += group_sum(g - 1, key)
        warp(g)
        key_end = key_at(g, 0)
        par = close(g - 1, key, par, key_end)
        return key_end, par

    key, par = lax.fori_loop(1, groups, step, (jnp.int32(low_key), jnp.int32(0)))
    total[par] += group_sum(groups - 1, key)
    close(groups - 1, key, par, low_key + keys)


def local_stacks(stage, patches, bits, sorted_args, offsets, coefs, tiles, mats):
    count, rows, cols = tiles.shape
    keys, half, wide = patches // 2, rows // 2, cols + LANES
    groups = -(-count // GROUP)
    smem = pl.BlockSpec(memory_space=pltpu.SMEM)
    vmem = pl.BlockSpec(memory_space=pltpu.VMEM)
    hbm = pl.BlockSpec(memory_space=pltpu.HBM)
    out_shape = [
        jax.ShapeDtypeStruct((keys, half, wide), BF16),
        jax.ShapeDtypeStruct((keys, half, wide), F32),
    ]
    out_specs = [vmem, vmem]
    scratch = [
        pltpu.VMEM((groups, GROUP, rows, cols), BF16),
        pltpu.VMEM((2, GROUP * rows, cols), BF16),
        pltpu.VMEM((2, BASES * rows, GROUP * rows), BF16),
        pltpu.VMEM((2, BASES * rows, cols), F32),
        pltpu.SemaphoreType.DMA((groups,)),
        pltpu.SMEM(offsets.shape, I32),
        pltpu.SMEM(coefs.shape, I32),
        *(pltpu.VMEM(m.shape, m.dtype) for m in mats),
        pltpu.SemaphoreType.DMA((2 + len(mats),)),
    ]
    in_specs = [hbm if stage == 0 else smem] * len(sorted_args)
    if stage == 0:
        out_shape += [
            jax.ShapeDtypeStruct((count,), I32),
            jax.ShapeDtypeStruct((count,), I32),
            jax.ShapeDtypeStruct((patches + 1,), I32),
            jax.ShapeDtypeStruct((count,), F32),
            jax.ShapeDtypeStruct((patches,), F32),
        ]
        out_specs += [smem] * 5
        scratch += [
            pltpu.SMEM((count,), I32),
            pltpu.VMEM((count,), BF16),
            pltpu.SMEM((patches,), I32),
            pltpu.VMEM((count,), F32),
            pltpu.SemaphoreType.DMA(()),
            pltpu.SemaphoreType.DMA((2,)),
        ]
    return pl.pallas_call(
        functools.partial(stack_kernel, stage, patches, bits),
        out_shape=tuple(out_shape),
        in_specs=[*in_specs] + [hbm] * (3 + len(mats)),
        out_specs=tuple(out_specs),
        scratch_shapes=scratch,
        cost_estimate=pl.CostEstimate(
            flops=2 * count * rows * cols * 4 * WIDE, bytes_accessed=count * rows * cols, transcendentals=0
        ),
    )(*sorted_args, offsets, coefs, tiles, *mats)


def merge_kernel(bits, near, *refs):
    mine, rim = refs[-2:]
    half, cols = mine.shape
    total = near[0]
    for got in refs[:-2]:
        total = total + got[...].astype(F32)
    digit_row = lax.broadcasted_iota(I32, (half, LANES), 0)
    live = digit_row * bits < WEIGHT_BITS + 30
    value = 2.0**WEIGHT_BITS / power_of_two((digit_row + 1) * bits)
    weight = jnp.sum(total[:, cols:] * jnp.where(live, value, 0.0), axis=0, keepdims=True)
    scale = 1.0 / jnp.sqrt(weight)
    upper = lax.axis_index("visit") == 0
    for b in range(cols // LANES):
        at = slice(b * LANES, (b + 1) * LANES)
        piece = total[:, at] * scale
        mine[:, at] = piece
        rim[:, at] = jnp.where(upper, piece[:HALO], piece[half - HALO :]).astype(BF16)


def smooth_kernel(rows_mat, cols_mat, mine, other, one, two, coadd, detection):
    half, cols = mine.shape
    blocks = cols // LANES
    rows = 2 * half
    upper = lax.axis_index("visit") == 0
    top = jnp.where(upper, mine[...], other[...])
    bottom = jnp.where(upper, other[...], mine[...])
    coadd[:half, :] = top
    coadd[half:, :] = bottom
    first, second = one[...].astype(F32), two[...].astype(F32)
    before = jnp.where(upper, second, first)
    after = jnp.where(upper, first, second)
    extended = jnp.concatenate([before, top, bottom, after], axis=0).astype(BF16)
    blurred = jnp.dot(rows_mat[...], extended, preferred_element_type=F32).astype(BF16)
    window = windows([block(blurred, b) for b in range(blocks)])
    result = jnp.dot(window, cols_mat[...], preferred_element_type=F32)
    for b in range(blocks):
        detection[:, b * LANES : (b + 1) * LANES] = result[b * rows : (b + 1) * rows]


def shards(visit_tiles, tile_patch, offsets, psf_coefs, weights):
    rows, cols = visit_tiles.shape[1:]
    owners = lax.axis_size("patch")
    keys, half = owners // 2, rows // 2
    bits = digit_bits(owners * lax.axis_size("visit"))
    mats = [jnp.asarray(m) for m in (lanczos_lines(), row_filters(rows), *psf_col_filters())]
    stacks = functools.partial(
        local_stacks,
        patches=owners,
        bits=bits,
        offsets=offsets.T,
        coefs=psf_coefs.T,
        tiles=visit_tiles,
        mats=mats,
    )
    swap = [(0, 1), (1, 0)]
    beside = [(i, i ^ 1) for i in range(owners)]
    send, keep, *sort = stacks(0, sorted_args=(tile_patch, weights))
    got = lax.ppermute(send, "visit", swap)
    far = (keep + got.astype(F32)).astype(BF16)
    crossed = lax.ppermute(far, "patch", beside)
    send, keep = stacks(1, sorted_args=sort)
    got = lax.ppermute(send, "visit", swap)
    near = keep + got.astype(F32) + crossed.astype(F32)
    sent = near.astype(BF16)
    parts = [
        lax.ppermute(sent[d], "patch", [(i, i ^ (2 * d)) for i in range(owners)]) for d in range(1, keys)
    ]
    mine, rim = pl.pallas_call(
        functools.partial(merge_kernel, bits),
        out_shape=(jax.ShapeDtypeStruct((half, cols), F32), jax.ShapeDtypeStruct((HALO, cols), BF16)),
        compiler_params=pltpu.CompilerParams(vmem_limit_bytes=8 << 20),
        name="merge",
    )(near[:1], *parts)
    pair = ("patch", "visit")
    up = [(2 * i + 1, 2 * i + 3) for i in range(owners - 1)]
    down = [(2 * i + 2, 2 * i) for i in range(owners - 1)]
    up_across = [(2 * i + 1, 2 * i + 2) for i in range(owners - 1)]
    down_across = [(2 * i + 2, 2 * i + 1) for i in range(owners - 1)]
    one = lax.ppermute(rim, pair, up + down)
    two = lax.ppermute(rim, pair, up_across + down_across)
    other = lax.ppermute(mine, "visit", swap)
    sigma = HALO / 4.0
    out_index = np.arange(rows, dtype=np.float64)[:, None]
    in_index = np.arange(rows + 2 * HALO, dtype=np.float64)[None, :]
    rows_mat = to_bf16(gaussian(out_index + HALO - in_index, sigma, HALO))
    return pl.pallas_call(
        smooth_kernel,
        out_shape=(jax.ShapeDtypeStruct((rows, cols), F32),) * 2,
        compiler_params=pltpu.CompilerParams(vmem_limit_bytes=8 << 20),
        name="smooth",
    )(jnp.asarray(rows_mat), jnp.asarray(col_filter(sigma, HALO)), mine, other, one, two)


def solution(mesh):
    placed = (
        P(("groups", "patch", "visit"), None, None),
        P(("groups", "patch", "visit")),
        P(("groups", "patch", "visit"), None),
        P(("groups", "patch", "visit"), None),
        P(("groups", "patch", "visit")),
    )

    return jax.shard_map(
        shards,
        mesh=mesh,
        in_specs=placed,
        out_specs=(P(("groups", "patch"), None), P(("groups", "patch"), None)),
        check_vma=False,
    )
```

```python
import functools
import math

import jax
import jax.numpy as jnp
import numpy as np
from jax import lax
from jax.experimental import pallas as pl
from jax.experimental.pallas import tpu as pltpu
from jax.sharding import PartitionSpec as P

BF16, F32, I32 = jnp.bfloat16, jnp.float32, jnp.int32
HALO = 8
PSF_SIGMAS = (0.75, 1.5, 3.0)
PSF_REACH = 16
BASES = len(PSF_SIGMAS)
LANES = 128
WIDE = 2 * LANES
GROUP = 4
PSF_BATCH = 4
STEPS = 64
OFFSET_MAX = 128
WEIGHT_BITS = 10
WARP_SEGMENT, WARP_EDGE = 32, 8
PSF_SEGMENT, PSF_EDGE = 64, 16


def gaussian(distance, sigma, reach):
    shape = np.exp(-distance * distance / (2.0 * sigma * sigma)) / (math.pi * sigma * sigma) ** 0.25
    return np.where(np.abs(distance) <= reach, shape, 0.0)


def to_bf16(value):
    return value.astype(np.float32).astype(BF16)


def row_filters(rows):
    index = np.arange(rows, dtype=np.float64)
    offset = index[:, None] - index[None, :]
    stacked = np.concatenate([gaussian(offset, s, PSF_REACH) for s in PSF_SIGMAS], axis=0)
    high = to_bf16(stacked)
    return np.concatenate([high, to_bf16(stacked - high.astype(np.float64))], axis=1)


def psf_col_filters():
    lane = np.arange(WIDE, dtype=np.float64)
    offset = lane[None, :] - lane[:, None]
    same = (lane[None, :] // PSF_SEGMENT) == (lane[:, None] // PSF_SEGMENT)
    bands = [gaussian(offset, s, PSF_REACH) for s in PSF_SIGMAS]
    main = np.concatenate(bands, axis=0)
    edge = np.concatenate([np.where(same, band, 0.0) for band in bands], axis=0)
    return to_bf16(main), to_bf16(edge)


def col_filter(sigma, reach):
    lane = np.arange(LANES, dtype=np.float64)
    offset = lane[None, :] - lane[:, None]
    wrapped = (offset + LANES // 2) % LANES - LANES // 2
    circulant = gaussian(wrapped, sigma, reach)
    own = np.where(np.abs(offset) < LANES // 2, circulant, 0.0)
    edge = np.where(np.abs(offset) >= LANES // 2, circulant, 0.0)
    return to_bf16(np.concatenate([own, edge], axis=0))


def lanczos_lines():
    lane = np.arange(LANES, dtype=np.float64)
    wrapped = (lane + LANES // 2) % LANES - LANES // 2
    offset = np.arange(-OFFSET_MAX, OFFSET_MAX + 8, dtype=np.float64)[:, None] / STEPS
    value = wrapped[None, :] + offset
    line = np.where(np.abs(value) < 3.0, np.sinc(value) * np.sinc(value / 3.0), 0.0)
    return line.astype(np.float32)


def digit_bits(devices):
    return max(1, int(math.log2(256 // devices)) if devices <= 128 else 1)


def power_of_two(exponent):
    out = 1.0
    for i in range(6):
        out = out * jnp.where((exponent >> i) & 1 == 1, 2.0 ** (2**i), 1.0)
    return out


def windows(blocks):
    rows = blocks[0].shape[0]
    left = lax.broadcasted_iota(I32, (rows, LANES), 1) < LANES // 2
    zero = jnp.zeros_like(blocks[0])
    padded = [zero, *blocks, zero]
    return jnp.concatenate(
        [
            jnp.concatenate([padded[b + 1], jnp.where(left, padded[b + 2], padded[b])], axis=1)
            for b in range(len(blocks))
        ],
        axis=0,
    )


def block(value, b):
    return value[:, b * LANES : (b + 1) * LANES]


def border_columns(value, segment):
    rows, cols = value.shape
    lane = lax.broadcasted_iota(I32, (rows, LANES), 1)
    per = LANES // segment
    borders = cols // WIDE - 1
    out = []
    for start in range(0, borders, per):
        merged = None
        for s in range(start, min(start + per, borders)):
            both = jnp.where(lane < LANES // 2, block(value, 2 * s + 2), block(value, 2 * s + 1))
            moved = pltpu.roll(both, segment // 2 + segment * (s - start), 1)
            merged = moved if merged is None else jnp.where(lane >= segment * (s - start), moved, merged)
        out.append(merged)
    return out


def mend_borders(blocks, edges, segment, reach):
    rows = blocks[0].shape[0]
    lane = lax.broadcasted_iota(I32, (rows, LANES), 1)
    per = LANES // segment
    blocks = list(blocks)
    for s in range(len(blocks) // 2 - 1):
        shift = LANES - segment // 2 - segment * (s % per)
        moved = pltpu.roll(edges[s // per], shift, 1)
        blocks[2 * s + 1] = jnp.where(lane >= LANES - reach, moved, blocks[2 * s + 1])
        blocks[2 * s + 2] = jnp.where(lane < reach, moved, blocks[2 * s + 2])
    return blocks


def side_by_side(value):
    return jnp.concatenate(
        [value[:, s : s + WIDE] for s in range(0, value.shape[1], WIDE)], axis=0
    )


def stack_kernel(
    bits,
    tile_patch_in,
    raw_weights_in,
    offsets_in,
    coefs_in,
    tiles,
    lines_in,
    row_mats_in,
    col_main_in,
    col_edge_in,
    send,
    keep,
    raw,
    shifted,
    mixers,
    total,
    stacked,
    strip,
    sems,
    tile_patch,
    raw_weights,
    offsets,
    coefs,
    lines,
    row_mats,
    col_main,
    col_edge,
    in_sems,
    weight_line,
    weight_sem,
    weights,
    weight_sq,
    order,
    first,
    cursor,
    rounded,
    out_sems,
):
    me = lax.axis_index("patch")
    helper = lax.axis_index("visit")
    count, rows, cols = tiles.shape
    patches = stacked.shape[0]
    near = (rows + 2 * HALO) // 2

    moves = [
        pltpu.make_async_copy(source, target, in_sems.at[i])
        for i, (source, target) in enumerate(
            (
                (tile_patch_in, tile_patch),
                (raw_weights_in, raw_weights),
                (offsets_in, offsets),
                (coefs_in, coefs),
                (lines_in, lines),
                (row_mats_in, row_mats),
                (col_main_in, col_main),
                (col_edge_in, col_edge),
            )
        )
    ]
    for move in moves:
        move.start()
    for k in range(patches):
        cursor[k] = 0
        weight_sq[k] = 0.0
    moves[0].wait()
    for t in range(count):
        cursor[tile_patch[t]] += 1
    running = 0
    for k in range(patches):
        number = cursor[k]
        first[k] = running
        cursor[k] = running
        running = running + number
    for t in range(count):
        key = tile_patch[t]
        slot = cursor[key]
        cursor[key] = slot + 1
        order[slot] = t

    groups = -(-count // GROUP)

    def tile_at(g, j):
        return order[jnp.minimum(g * GROUP + j, count - 1)]

    def key_at(g, j):
        slot = g * GROUP + j
        key = tile_patch[order[jnp.minimum(slot, count - 1)]]
        return key if count % GROUP == 0 else jnp.where(slot < count, key, -1)

    def fetch(g, carry):
        for j in range(GROUP):
            pltpu.make_async_copy(tiles.at[tile_at(g, j)], raw.at[g, j], sems.at[g]).start()
        return carry

    lax.fori_loop(0, groups, fetch, 0)

    moves[1].wait()
    weight_line[...] = raw_weights[...].astype(F32)
    weight_copy = pltpu.make_async_copy(weight_line, weights, weight_sem)
    weight_copy.start()
    strip[...] = jnp.zeros_like(strip)
    weight_copy.wait()
    for t in range(count):
        weight_sq[tile_patch[t]] += weights[t] * weights[t]

    square = lax.broadcasted_iota(I32, (LANES, LANES), 1) - lax.broadcasted_iota(I32, (LANES, LANES), 0)
    ahead, behind = square <= -LANES // 2, square >= LANES // 2
    inner = jnp.abs(square) < LANES // 2
    segment_of = lambda axis: lax.broadcasted_iota(I32, (LANES, LANES), axis) // WARP_SEGMENT
    same_segment = segment_of(0) == segment_of(1)
    half_lanes = lax.broadcasted_iota(I32, (rows, LANES), 1) < LANES // 2
    half_row = lax.broadcasted_iota(I32, (1, LANES), 1) < LANES // 2

    def band(line, height):
        spread = jnp.broadcast_to(line, (height, LANES))
        return pltpu.roll(spread, 0, 1, stride=1, stride_axis=0)

    def line_of(offset):
        return lines[pl.ds(jnp.clip(offset + OFFSET_MAX, 0, 2 * OFFSET_MAX), 1), :]

    def arrive(g):
        pltpu.make_async_copy(tiles.at[pl.ds(0, GROUP)], raw.at[g], sems.at[g]).wait()

    def warp(g):
        slot = g & 1
        ids = [tile_at(g, j) for j in range(GROUP)]
        for j in range(0, GROUP, 2):
            spreads, ends, end_mats = [], [], []
            for i in range(2):
                circulant = band(line_of(offsets[1, ids[j + i]]), LANES)
                pick = lambda mask: jnp.where(mask, circulant, 0.0).astype(BF16)
                own = pick(inner)
                spreads.append(
                    jnp.concatenate(
                        [
                            jnp.concatenate([own, pick(ahead)], axis=1),
                            jnp.concatenate([pick(behind), own], axis=1),
                        ],
                        axis=0,
                    )
                )
                ends.append(border_columns(raw[g, j + i], WARP_SEGMENT)[0])
                end_mats.append(pick(same_segment))
            empty = jnp.zeros((LANES, LANES), BF16)
            mats = jnp.concatenate(
                [
                    jnp.concatenate([end_mats[0], empty], axis=1),
                    jnp.concatenate([empty, end_mats[1]], axis=1),
                ],
                axis=0,
            )
            mended = jnp.dot(
                jnp.concatenate(ends, axis=1), mats, preferred_element_type=F32
            ).astype(BF16)
            for i in range(2):
                value = jnp.dot(
                    side_by_side(raw[g, j + i]), spreads[i], preferred_element_type=F32
                ).astype(BF16)
                blocks = [
                    block(value[s * rows : (s + 1) * rows], b) for s in range(cols // WIDE) for b in range(2)
                ]
                blocks = mend_borders(blocks, [block(mended, i)], WARP_SEGMENT, WARP_EDGE)
                for b, piece in enumerate(blocks):
                    shifted[slot, (j + i) * rows : (j + i + 1) * rows, b * LANES : (b + 1) * LANES] = piece
        pairs = []
        for j in range(0, GROUP, 2):
            one = band(line_of(-offsets[0, ids[j]]), rows)
            two = band(pltpu.roll(line_of(-offsets[0, ids[j + 1]]), LANES // 2, 1), rows)
            pairs.append(jnp.where(half_lanes, one, two).astype(BF16))
        mixer = jnp.concatenate(pairs, axis=1)
        mixer = jnp.concatenate([mixer, mixer], axis=0)
        mixer = jnp.dot(row_mats[...], mixer, preferred_element_type=F32)
        for k in range(BASES):
            scales = [weights[t] * (coefs[k, t].astype(F32) / STEPS) for t in ids]
            scale = jnp.concatenate(
                [jnp.where(half_row, scales[j], scales[j + 1]) for j in range(0, GROUP, 2)], axis=1
            )
            mixers[slot, k * rows : (k + 1) * rows, :] = (mixer[k * rows : (k + 1) * rows] * scale).astype(BF16)

    def group_sum(g, key):
        slot = g & 1
        owner = jnp.concatenate(
            [jnp.where(half_row, key_at(g, j), key_at(g, j + 1)) for j in range(0, GROUP, 2)], axis=1
        )
        mixer = jnp.where(owner == key, mixers[slot], jnp.zeros((), BF16))
        return jnp.dot(mixer, shifted[slot], preferred_element_type=F32)

    def close(g, key, key_end):
        def one(k, carry):
            stacked[k] = total[...].astype(BF16)
            total[...] = group_sum(g, k + 1)
            return carry

        lax.fori_loop(key, key_end, one, 0)

    for move in moves[2:]:
        move.wait()
    total[...] = jnp.zeros_like(total)
    arrive(0)
    warp(0)

    def step(g, key):
        arrive(g)
        total[...] += group_sum(g - 1, key)
        warp(g)
        key_end = key_at(g, 0)
        close(g - 1, key, key_end)
        return key_end

    key = lax.fori_loop(1, groups, step, jnp.int32(0))
    total[...] += group_sum(groups - 1, key)
    close(groups - 1, key, patches)

    lane = lax.broadcasted_iota(I32, (rows, LANES), 1)
    digit_live = lane * bits < WEIGHT_BITS + 30
    scale_up = jnp.where(digit_live, power_of_two((lane + 1) * bits) * 2.0**-WEIGHT_BITS, 0.0)

    def match(q):
        mains, edges = [], []
        for k in range(BASES):
            base_k = stacked[q, k * rows : (k + 1) * rows, :]
            mains.append(side_by_side(base_k))
            edges.extend(border_columns(base_k, PSF_SEGMENT))
        edge = jnp.dot(jnp.concatenate(edges, axis=1), col_edge[...], preferred_element_type=F32)
        main = jnp.dot(jnp.concatenate(mains, axis=1), col_main[...], preferred_element_type=F32)
        blocks = [block(main[s * rows : (s + 1) * rows], b) for s in range(cols // WIDE) for b in range(2)]
        blocks = mend_borders(blocks, [block(edge, 0), block(edge, 1)], PSF_SEGMENT, PSF_EDGE)
        at = pl.ds(pl.multiple_of(HALO + q * rows, 8), rows)
        for b, piece in enumerate(blocks):
            strip[at, b * LANES : (b + 1) * LANES] = piece
        scaled = jnp.floor(weight_sq[q] * scale_up)
        strip[at, cols:] = scaled - 2.0**bits * jnp.floor(scaled * 2.0**-bits)

    batch = math.gcd(patches, PSF_BATCH)

    def match_some(i, carry):
        for j in range(batch):
            match(i * batch + j)
        return carry

    lax.fori_loop(0, patches // batch, match_some, 0)

    def hand_out(d, carry):
        q = d ^ me
        own = pl.ds(pl.multiple_of(q * rows + helper * near, 8), near)
        other = pl.ds(pl.multiple_of(q * rows + (1 - helper) * near, 8), near)
        pltpu.make_async_copy(strip.at[own], keep.at[d], out_sems.at[0]).start()
        rounded[d] = strip[other, :].astype(BF16)
        pltpu.make_async_copy(rounded.at[d], send.at[d], out_sems.at[1]).start()
        return carry

    lax.fori_loop(0, patches, hand_out, 0)
    pltpu.make_async_copy(keep, keep, out_sems.at[0]).wait()
    pltpu.make_async_copy(rounded, send, out_sems.at[1]).wait()


def local_stacks(patches, bits, tile_patch, weights, offsets, coefs, tiles, mats):
    count, rows, cols = tiles.shape
    near, wide = (rows + 2 * HALO) // 2, cols + LANES
    groups = -(-count // GROUP)
    hbm = pl.BlockSpec(memory_space=pltpu.HBM)
    return pl.pallas_call(
        functools.partial(stack_kernel, bits),
        out_shape=(
            jax.ShapeDtypeStruct((patches, near, wide), BF16),
            jax.ShapeDtypeStruct((patches, near, wide), F32),
        ),
        in_specs=[hbm] * (5 + len(mats)),
        out_specs=(hbm, hbm),
        scratch_shapes=[
            pltpu.VMEM((groups, GROUP, rows, cols), BF16),
            pltpu.VMEM((2, GROUP * rows, cols), BF16),
            pltpu.VMEM((2, BASES * rows, GROUP * rows), BF16),
            pltpu.VMEM((BASES * rows, cols), F32),
            pltpu.VMEM((patches, BASES * rows, cols), BF16),
            pltpu.VMEM((patches * rows + 2 * HALO, wide), F32),
            pltpu.SemaphoreType.DMA((groups,)),
            pltpu.SMEM((count,), I32),
            pltpu.VMEM((count,), BF16),
            pltpu.SMEM(offsets.shape, I32),
            pltpu.SMEM(coefs.shape, I32),
            *(pltpu.VMEM(m.shape, m.dtype) for m in mats),
            pltpu.SemaphoreType.DMA((4 + len(mats),)),
            pltpu.VMEM((count,), F32),
            pltpu.SemaphoreType.DMA(()),
            pltpu.SMEM((count,), F32),
            pltpu.SMEM((patches,), F32),
            pltpu.SMEM((count,), I32),
            pltpu.SMEM((patches,), I32),
            pltpu.SMEM((patches,), I32),
            pltpu.VMEM((patches, near, wide), BF16),
            pltpu.SemaphoreType.DMA((2,)),
        ],
        cost_estimate=pl.CostEstimate(
            flops=2 * count * rows * cols * 4 * WIDE, bytes_accessed=count * rows * cols, transcendentals=0
        ),
        name="stacks",
    )(tile_patch, weights, offsets, coefs, tiles, *mats)


def merge_kernel(bits, *refs):
    mine = refs[-1]
    cols = mine.shape[1]
    total = refs[0][...]
    for got in refs[1:-1]:
        total = total + got[...].astype(F32)
    digits = total[:, cols:]
    lane = lax.broadcasted_iota(I32, digits.shape, 1)
    live = lane * bits < WEIGHT_BITS + 30
    value = jnp.where(live, 2.0**WEIGHT_BITS / power_of_two((lane + 1) * bits), 0.0)
    weight = jnp.sum(digits * value, axis=1, keepdims=True)
    scale = jnp.where(weight > 0.0, 1.0 / jnp.sqrt(jnp.where(weight > 0.0, weight, 1.0)), 0.0)
    mine[...] = total[:, :cols] * scale


def smooth_kernel(rows_mat, cols_mat, mine, other, coadd, detection):
    near, cols = mine.shape
    rows = coadd.shape[0]
    upper = lax.axis_index("visit") == 0
    top = jnp.where(upper, mine[...], other[...])
    bottom = jnp.where(upper, other[...], mine[...])
    coadd[: near - HALO, :] = top[HALO:]
    coadd[near - HALO :, :] = bottom[: near - HALO]
    extended = jnp.concatenate([top, bottom], axis=0).astype(BF16)
    blurred = jnp.dot(rows_mat[...], extended, preferred_element_type=F32).astype(BF16)
    blocks = cols // LANES
    window = windows([block(blurred, b) for b in range(blocks)])
    result = jnp.dot(window, cols_mat[...], preferred_element_type=F32)
    for b in range(blocks):
        detection[:, b * LANES : (b + 1) * LANES] = result[b * rows : (b + 1) * rows]


def shards(visit_tiles, tile_patch, offsets, psf_coefs, weights):
    rows, cols = visit_tiles.shape[1:]
    owners = lax.axis_size("patch")
    near, wide = (rows + 2 * HALO) // 2, cols + LANES
    bits = digit_bits(owners * lax.axis_size("visit"))
    mats = [jnp.asarray(m) for m in (lanczos_lines(), row_filters(rows), *psf_col_filters())]
    send, keep = local_stacks(
        owners, bits, tile_patch, weights, offsets.T, psf_coefs.T, visit_tiles, mats
    )
    swap = [(0, 1), (1, 0)]
    both = keep + lax.ppermute(send, "visit", swap).astype(F32)
    sent = both.astype(BF16)
    parts = [both[0]] + [
        lax.ppermute(sent[d], "patch", [(i, i ^ d) for i in range(owners)]) for d in range(owners - 1, 0, -1)
    ]
    mine = pl.pallas_call(
        functools.partial(merge_kernel, bits),
        out_shape=jax.ShapeDtypeStruct((near, cols), F32),
        compiler_params=pltpu.CompilerParams(vmem_limit_bytes=16 << 20),
        name="merge",
    )(*parts)
    other = lax.ppermute(mine, "visit", swap)
    sigma = HALO / 4.0
    out_index = np.arange(rows, dtype=np.float64)[:, None]
    in_index = np.arange(rows + 2 * HALO, dtype=np.float64)[None, :]
    rows_mat = to_bf16(gaussian(out_index + HALO - in_index, sigma, HALO))
    return pl.pallas_call(
        smooth_kernel,
        out_shape=(jax.ShapeDtypeStruct((rows, cols), F32),) * 2,
        compiler_params=pltpu.CompilerParams(vmem_limit_bytes=8 << 20),
        name="smooth",
    )(jnp.asarray(rows_mat), jnp.asarray(col_filter(sigma, HALO)), mine, other)


def solution(mesh):
    placed = (
        P(("groups", "patch", "visit"), None, None),
        P(("groups", "patch", "visit")),
        P(("groups", "patch", "visit"), None),
        P(("groups", "patch", "visit"), None),
        P(("groups", "patch", "visit")),
    )
    return jax.shard_map(
        shards,
        mesh=mesh,
        in_specs=placed,
        out_specs=(P(("groups", "patch"), None), P(("groups", "patch"), None)),
        check_vma=False,
    )
```

```python
import functools
import math

import jax
import jax.numpy as jnp
import numpy as np
from jax import lax
from jax.experimental import pallas as pl
from jax.experimental.pallas import tpu as pltpu
from jax.sharding import PartitionSpec as P


BF16, F32, I32 = jnp.bfloat16, jnp.float32, jnp.int32
HALO = 8
PSF_SIGMAS = (0.75, 1.5, 3.0)
PSF_REACH = 16
BASES = len(PSF_SIGMAS)
LANES = 128
WIDE = 2 * LANES
GROUP = 4
PSF_BATCH = 4
STEPS = 64
OFFSET_MAX = 128
WEIGHT_BITS = 10
WARP_SEGMENT, WARP_EDGE = 32, 8
PSF_SEGMENT, PSF_EDGE = 64, 16


def gaussian(distance, sigma, reach):
    shape = np.exp(-distance * distance / (2.0 * sigma * sigma)) / (math.pi * sigma * sigma) ** 0.25
    return np.where(np.abs(distance) <= reach, shape, 0.0)


def to_bf16(value):
    return value.astype(np.float32).astype(BF16)


def row_filters(rows):
    index = np.arange(rows, dtype=np.float64)
    offset = index[:, None] - index[None, :]
    stacked = np.concatenate([gaussian(offset, s, PSF_REACH) for s in PSF_SIGMAS], axis=0)
    high = to_bf16(stacked)
    return np.concatenate([high, to_bf16(stacked - high.astype(np.float64))], axis=1)


def psf_col_filters():
    lane = np.arange(WIDE, dtype=np.float64)
    offset = lane[None, :] - lane[:, None]
    same = (lane[None, :] // PSF_SEGMENT) == (lane[:, None] // PSF_SEGMENT)
    bands = [gaussian(offset, s, PSF_REACH) for s in PSF_SIGMAS]
    main = np.concatenate(bands, axis=0)
    edge = np.concatenate([np.where(same, band, 0.0) for band in bands], axis=0)
    return to_bf16(main), to_bf16(edge)


def col_filter(sigma, reach):
    lane = np.arange(LANES, dtype=np.float64)
    offset = lane[None, :] - lane[:, None]
    wrapped = (offset + LANES // 2) % LANES - LANES // 2
    circulant = gaussian(wrapped, sigma, reach)
    own = np.where(np.abs(offset) < LANES // 2, circulant, 0.0)
    edge = np.where(np.abs(offset) >= LANES // 2, circulant, 0.0)
    return to_bf16(np.concatenate([own, edge], axis=0))


def lanczos_lines():
    lane = np.arange(LANES, dtype=np.float64)
    wrapped = (lane + LANES // 2) % LANES - LANES // 2
    offset = np.arange(-OFFSET_MAX, OFFSET_MAX + 8, dtype=np.float64)[:, None] / STEPS
    value = wrapped[None, :] + offset
    line = np.where(np.abs(value) < 3.0, np.sinc(value) * np.sinc(value / 3.0), 0.0)
    return line.astype(np.float32)


def digit_bits(devices):
    return max(1, int(math.log2(256 // devices)) if devices <= 128 else 1)


def power_of_two(exponent):
    out = 1.0
    for i in range(6):
        out = out * jnp.where((exponent >> i) & 1 == 1, 2.0 ** (2**i), 1.0)
    return out


def windows(blocks):
    rows = blocks[0].shape[0]
    left = lax.broadcasted_iota(I32, (rows, LANES), 1) < LANES // 2
    zero = jnp.zeros_like(blocks[0])
    padded = [zero, *blocks, zero]
    return jnp.concatenate(
        [
            jnp.concatenate([padded[b + 1], jnp.where(left, padded[b + 2], padded[b])], axis=1)
            for b in range(len(blocks))
        ],
        axis=0,
    )


def block(value, b):
    return value[:, b * LANES : (b + 1) * LANES]


def border_columns(value, segment):
    rows, cols = value.shape
    lane = lax.broadcasted_iota(I32, (rows, LANES), 1)
    per = LANES // segment
    borders = cols // WIDE - 1
    out = []
    for start in range(0, borders, per):
        merged = None
        for s in range(start, min(start + per, borders)):
            both = jnp.where(lane < LANES // 2, block(value, 2 * s + 2), block(value, 2 * s + 1))
            moved = pltpu.roll(both, segment // 2 + segment * (s - start), 1)
            merged = moved if merged is None else jnp.where(lane >= segment * (s - start), moved, merged)
        out.append(merged)
    return out


def mend_borders(blocks, edges, segment, reach):
    rows = blocks[0].shape[0]
    lane = lax.broadcasted_iota(I32, (rows, LANES), 1)
    per = LANES // segment
    blocks = list(blocks)
    for s in range(len(blocks) // 2 - 1):
        shift = LANES - segment // 2 - segment * (s % per)
        moved = pltpu.roll(edges[s // per], shift, 1)
        blocks[2 * s + 1] = jnp.where(lane >= LANES - reach, moved, blocks[2 * s + 1])
        blocks[2 * s + 2] = jnp.where(lane < reach, moved, blocks[2 * s + 2])
    return blocks


def side_by_side(value):
    return jnp.concatenate(
        [value[:, s : s + WIDE] for s in range(0, value.shape[1], WIDE)], axis=0
    )


def stack_kernel(
    bits,
    tile_patch_in,
    raw_weights_in,
    offsets_in,
    coefs_in,
    tiles,
    lines_in,
    row_mats_in,
    col_main_in,
    col_edge_in,
    first_send,
    rest_send,
    first_keep,
    rest_keep,
    raw,
    shifted,
    mixers,
    total,
    stacked,
    strip,
    sems,
    tile_patch,
    raw_weights,
    offsets,
    coefs,
    lines,
    row_mats,
    col_main,
    col_edge,
    in_sems,
    weight_line,
    weight_sem,
    weights,
    weight_sq,
    order,
    first,
    cursor,
    rounded,
    out_sems,
):
    me = lax.axis_index("patch")
    helper = lax.axis_index("visit")
    count, rows, cols = tiles.shape
    patches = stacked.shape[0]
    near = (rows + 2 * HALO) // 2

    moves = [
        pltpu.make_async_copy(source, target, in_sems.at[i])
        for i, (source, target) in enumerate(
            (
                (tile_patch_in, tile_patch),
                (raw_weights_in, raw_weights),
                (offsets_in, offsets),
                (coefs_in, coefs),
                (lines_in, lines),
                (row_mats_in, row_mats),
                (col_main_in, col_main),
                (col_edge_in, col_edge),
            )
        )
    ]
    for move in moves:
        move.start()
    for k in range(patches):
        cursor[k] = 0
        weight_sq[k] = 0.0
    moves[0].wait()
    for t in range(count):
        cursor[tile_patch[t]] += 1
    running = 0
    for k in range(patches):
        number = cursor[k]
        first[k] = running
        cursor[k] = running
        running = running + number
    for t in range(count):
        key = tile_patch[t]
        slot = cursor[key]
        cursor[key] = slot + 1
        order[slot] = t

    groups = -(-count // GROUP)

    def tile_at(g, j):
        return order[jnp.minimum(g * GROUP + j, count - 1)]

    def key_at(g, j):
        slot = g * GROUP + j
        key = tile_patch[order[jnp.minimum(slot, count - 1)]]
        return key if count % GROUP == 0 else jnp.where(slot < count, key, -1)

    def fetch(g, carry):
        for j in range(GROUP):
            pltpu.make_async_copy(tiles.at[tile_at(g, j)], raw.at[g, j], sems.at[g]).start()
        return carry

    lax.fori_loop(0, groups, fetch, 0)

    moves[1].wait()
    weight_line[...] = raw_weights[...].astype(F32)
    weight_copy = pltpu.make_async_copy(weight_line, weights, weight_sem)
    weight_copy.start()
    strip[...] = jnp.zeros_like(strip)
    weight_copy.wait()
    for t in range(count):
        weight_sq[tile_patch[t]] += weights[t] * weights[t]

    square = lax.broadcasted_iota(I32, (LANES, LANES), 1) - lax.broadcasted_iota(I32, (LANES, LANES), 0)
    ahead, behind = square <= -LANES // 2, square >= LANES // 2
    inner = jnp.abs(square) < LANES // 2
    segment_of = lambda axis: lax.broadcasted_iota(I32, (LANES, LANES), axis) // WARP_SEGMENT
    same_segment = segment_of(0) == segment_of(1)
    half_lanes = lax.broadcasted_iota(I32, (rows, LANES), 1) < LANES // 2
    half_row = lax.broadcasted_iota(I32, (1, LANES), 1) < LANES // 2

    def band(line, height):
        spread = jnp.broadcast_to(line, (height, LANES))
        return pltpu.roll(spread, 0, 1, stride=1, stride_axis=0)

    def line_of(offset):
        return lines[pl.ds(jnp.clip(offset + OFFSET_MAX, 0, 2 * OFFSET_MAX), 1), :]

    def arrive(g):
        pltpu.make_async_copy(tiles.at[pl.ds(0, GROUP)], raw.at[g], sems.at[g]).wait()

    def warp(g):
        slot = g & 1
        ids = [tile_at(g, j) for j in range(GROUP)]
        for j in range(0, GROUP, 2):
            spreads, ends, end_mats = [], [], []
            for i in range(2):
                circulant = band(line_of(offsets[1, ids[j + i]]), LANES)
                pick = lambda mask: jnp.where(mask, circulant, 0.0).astype(BF16)
                own = pick(inner)
                spreads.append(
                    jnp.concatenate(
                        [
                            jnp.concatenate([own, pick(ahead)], axis=1),
                            jnp.concatenate([pick(behind), own], axis=1),
                        ],
                        axis=0,
                    )
                )
                ends.append(border_columns(raw[g, j + i], WARP_SEGMENT)[0])
                end_mats.append(pick(same_segment))
            empty = jnp.zeros((LANES, LANES), BF16)
            mats = jnp.concatenate(
                [
                    jnp.concatenate([end_mats[0], empty], axis=1),
                    jnp.concatenate([empty, end_mats[1]], axis=1),
                ],
                axis=0,
            )
            mended = jnp.dot(
                jnp.concatenate(ends, axis=1), mats, preferred_element_type=F32
            ).astype(BF16)
            for i in range(2):
                value = jnp.dot(
                    side_by_side(raw[g, j + i]), spreads[i], preferred_element_type=F32
                ).astype(BF16)
                blocks = [
                    block(value[s * rows : (s + 1) * rows], b) for s in range(cols // WIDE) for b in range(2)
                ]
                blocks = mend_borders(blocks, [block(mended, i)], WARP_SEGMENT, WARP_EDGE)
                for b, piece in enumerate(blocks):
                    shifted[slot, (j + i) * rows : (j + i + 1) * rows, b * LANES : (b + 1) * LANES] = piece
        pairs = []
        for j in range(0, GROUP, 2):
            one = band(line_of(-offsets[0, ids[j]]), rows)
            two = band(pltpu.roll(line_of(-offsets[0, ids[j + 1]]), LANES // 2, 1), rows)
            pairs.append(jnp.where(half_lanes, one, two).astype(BF16))
        mixer = jnp.concatenate(pairs, axis=1)
        mixer = jnp.concatenate([mixer, mixer], axis=0)
        mixer = jnp.dot(row_mats[...], mixer, preferred_element_type=F32)
        for k in range(BASES):
            scales = [weights[t] * (coefs[k, t].astype(F32) / STEPS) for t in ids]
            scale = jnp.concatenate(
                [jnp.where(half_row, scales[j], scales[j + 1]) for j in range(0, GROUP, 2)], axis=1
            )
            mixers[slot, k * rows : (k + 1) * rows, :] = (mixer[k * rows : (k + 1) * rows] * scale).astype(BF16)

    def group_sum(g, key):
        slot = g & 1
        owner = jnp.concatenate(
            [jnp.where(half_row, key_at(g, j), key_at(g, j + 1)) for j in range(0, GROUP, 2)], axis=1
        )
        mixer = jnp.where(owner == key, mixers[slot], jnp.zeros((), BF16))
        return jnp.dot(mixer, shifted[slot], preferred_element_type=F32)

    def close(g, key, key_end):
        def one(k, carry):
            stacked[k] = total[...].astype(BF16)
            total[...] = group_sum(g, k + 1)
            return carry

        lax.fori_loop(key, key_end, one, 0)

    for move in moves[2:]:
        move.wait()
    total[...] = jnp.zeros_like(total)
    arrive(0)
    warp(0)

    def step(g, key):
        arrive(g)
        total[...] += group_sum(g - 1, key)
        warp(g)
        key_end = key_at(g, 0)
        close(g - 1, key, key_end)
        return key_end

    key = lax.fori_loop(1, groups, step, jnp.int32(0))
    total[...] += group_sum(groups - 1, key)
    close(groups - 1, key, patches)

    lane = lax.broadcasted_iota(I32, (rows, LANES), 1)
    digit_live = lane * bits < WEIGHT_BITS + 30
    scale_up = jnp.where(digit_live, power_of_two((lane + 1) * bits) * 2.0**-WEIGHT_BITS, 0.0)

    def match(q):
        mains, edges = [], []
        for k in range(BASES):
            base_k = stacked[q, k * rows : (k + 1) * rows, :]
            mains.append(side_by_side(base_k))
            edges.extend(border_columns(base_k, PSF_SEGMENT))
        edge = jnp.dot(jnp.concatenate(edges, axis=1), col_edge[...], preferred_element_type=F32)
        main = jnp.dot(jnp.concatenate(mains, axis=1), col_main[...], preferred_element_type=F32)
        blocks = [block(main[s * rows : (s + 1) * rows], b) for s in range(cols // WIDE) for b in range(2)]
        blocks = mend_borders(blocks, [block(edge, 0), block(edge, 1)], PSF_SEGMENT, PSF_EDGE)
        at = pl.ds(pl.multiple_of(HALO + q * rows, 8), rows)
        for b, piece in enumerate(blocks):
            strip[at, b * LANES : (b + 1) * LANES] = piece
        scaled = jnp.floor(weight_sq[q] * scale_up)
        strip[at, cols:] = scaled - 2.0**bits * jnp.floor(scaled * 2.0**-bits)

    batch = math.gcd(patches, PSF_BATCH)

    def match_some(i, carry):
        for j in range(batch):
            match(i * batch + j)
        return carry

    lax.fori_loop(0, patches // batch, match_some, 0)

    pairs = patches // 2
    early = first_send.shape[0]

    def hand_out(start, send, keep):
        def one(i, carry):
            d = start + i
            q = me ^ (2 * ((d + pairs // 2) % pairs) + jnp.where(d < pairs, 1, 0))
            own = pl.ds(pl.multiple_of(q * rows + helper * near, 8), near)
            other = pl.ds(pl.multiple_of(q * rows + (1 - helper) * near, 8), near)
            rounded[d] = strip[other, :].astype(BF16)
            pltpu.make_async_copy(rounded.at[d], send.at[i], out_sems.at[0]).start()
            pltpu.make_async_copy(strip.at[own], keep.at[i], out_sems.at[1]).start()
            return carry

        lax.fori_loop(0, send.shape[0], one, 0)

    hand_out(0, first_send, first_keep)
    hand_out(early, rest_send, rest_keep)
    pltpu.make_async_copy(rounded, rounded, out_sems.at[0]).wait()
    kept = strip.at[pl.ds(0, patches * near)]
    pltpu.make_async_copy(kept, kept, out_sems.at[1]).wait()


def local_stacks(patches, bits, tile_patch, weights, offsets, coefs, tiles, mats):
    count, rows, cols = tiles.shape
    near, wide = (rows + 2 * HALO) // 2, cols + LANES
    groups = -(-count // GROUP)
    hbm = pl.BlockSpec(memory_space=pltpu.HBM)
    return pl.pallas_call(
        functools.partial(stack_kernel, bits),
        out_shape=tuple(
            jax.ShapeDtypeStruct((number, near, wide), kind)
            for kind in (BF16, F32)
            for number in (patches // 4, patches - patches // 4)
        ),
        in_specs=[hbm] * (5 + len(mats)),
        out_specs=(hbm,) * 4,
        scratch_shapes=[
            pltpu.VMEM((groups, GROUP, rows, cols), BF16),
            pltpu.VMEM((2, GROUP * rows, cols), BF16),
            pltpu.VMEM((2, BASES * rows, GROUP * rows), BF16),
            pltpu.VMEM((BASES * rows, cols), F32),
            pltpu.VMEM((patches, BASES * rows, cols), BF16),
            pltpu.VMEM((patches * rows + 2 * HALO, wide), F32),
            pltpu.SemaphoreType.DMA((groups,)),
            pltpu.SMEM((count,), I32),
            pltpu.VMEM((count,), BF16),
            pltpu.SMEM(offsets.shape, I32),
            pltpu.SMEM(coefs.shape, I32),
            *(pltpu.VMEM(m.shape, m.dtype) for m in mats),
            pltpu.SemaphoreType.DMA((4 + len(mats),)),
            pltpu.VMEM((count,), F32),
            pltpu.SemaphoreType.DMA(()),
            pltpu.SMEM((count,), F32),
            pltpu.SMEM((patches,), F32),
            pltpu.SMEM((count,), I32),
            pltpu.SMEM((patches,), I32),
            pltpu.SMEM((patches,), I32),
            pltpu.VMEM((patches, near, wide), BF16),
            pltpu.SemaphoreType.DMA((2,)),
        ],
        cost_estimate=pl.CostEstimate(
            flops=2 * count * rows * cols * 4 * WIDE, bytes_accessed=count * rows * cols, transcendentals=0
        ),
        name="stacks",
    )(tile_patch, weights, offsets, coefs, tiles, *mats)


def merge_kernel(bits, *refs):
    mine = refs[-1]
    cols = mine.shape[1]
    total = refs[0][...]
    for got in refs[1:-1]:
        total = total + got[...].astype(F32)
    digits = total[:, cols:]
    lane = lax.broadcasted_iota(I32, digits.shape, 1)
    live = lane * bits < WEIGHT_BITS + 30
    value = jnp.where(live, 2.0**WEIGHT_BITS / power_of_two((lane + 1) * bits), 0.0)
    weight = jnp.sum(digits * value, axis=1, keepdims=True)
    scale = jnp.where(weight > 0.0, 1.0 / jnp.sqrt(jnp.where(weight > 0.0, weight, 1.0)), 0.0)
    mine[...] = total[:, :cols] * scale


def smooth_kernel(rows_mat, cols_mat, mine, other, coadd, detection):
    near, cols = mine.shape
    rows = coadd.shape[0]
    upper = lax.axis_index("visit") == 0
    top = jnp.where(upper, mine[...], other[...])
    bottom = jnp.where(upper, other[...], mine[...])
    coadd[: near - HALO, :] = top[HALO:]
    coadd[near - HALO :, :] = bottom[: near - HALO]
    extended = jnp.concatenate([top, bottom], axis=0).astype(BF16)
    blurred = jnp.dot(rows_mat[...], extended, preferred_element_type=F32).astype(BF16)
    blocks = cols // LANES
    window = windows([block(blurred, b) for b in range(blocks)])
    result = jnp.dot(window, cols_mat[...], preferred_element_type=F32)
    for b in range(blocks):
        detection[:, b * LANES : (b + 1) * LANES] = result[b * rows : (b + 1) * rows]


def shards(visit_tiles, tile_patch, offsets, psf_coefs, weights):
    rows, cols = visit_tiles.shape[1:]
    owners = lax.axis_size("patch")
    near = (rows + 2 * HALO) // 2
    bits = digit_bits(owners * lax.axis_size("visit"))
    mats = [jnp.asarray(m) for m in (lanczos_lines(), row_filters(rows), *psf_col_filters())]
    first_send, rest_send, first_keep, rest_keep = local_stacks(
        owners, bits, tile_patch, weights, offsets.T, psf_coefs.T, visit_tiles, mats
    )
    swap = [(0, 1), (1, 0)]
    beside = [(i, i ^ 1) for i in range(owners)]
    pairs = owners // 2
    cut = pairs // 2
    first_sum = (first_keep + lax.ppermute(first_send, "visit", swap).astype(F32)).astype(BF16)
    rest = rest_keep + lax.ppermute(rest_send, "visit", swap).astype(F32)
    evens = rest[pairs - cut :]
    bounds = sorted({0, cut // 2, cut, pairs})
    parts = [evens[cut]]
    for c, (low, high) in enumerate(zip(bounds[:-1], bounds[1:], strict=True)):
        crossing = first_sum[low:high] if high <= cut else rest[low - cut : high - cut].astype(BF16)
        crossed = lax.ppermute(crossing, "patch", beside)
        local = evens[low:high] if c == 0 else lax.optimization_barrier(evens[low:high])
        for i in range(low, high):
            e = (i + cut) % pairs
            if e == 0:
                parts.append(crossed[i - low])
            else:
                hop = [(j, j ^ (2 * e)) for j in range(owners)]
                summed = (local[i - low] + crossed[i - low].astype(F32)).astype(BF16)
                parts.append(lax.ppermute(summed, "patch", hop))
    mine = pl.pallas_call(
        functools.partial(merge_kernel, bits),
        out_shape=jax.ShapeDtypeStruct((near, cols), F32),
        compiler_params=pltpu.CompilerParams(vmem_limit_bytes=16 << 20),
        name="merge",
    )(*parts)
    other = lax.ppermute(mine, "visit", swap)
    sigma = HALO / 4.0
    out_index = np.arange(rows, dtype=np.float64)[:, None]
    in_index = np.arange(rows + 2 * HALO, dtype=np.float64)[None, :]
    rows_mat = to_bf16(gaussian(out_index + HALO - in_index, sigma, HALO))
    return pl.pallas_call(
        smooth_kernel,
        out_shape=(jax.ShapeDtypeStruct((rows, cols), F32),) * 2,
        compiler_params=pltpu.CompilerParams(vmem_limit_bytes=8 << 20),
        name="smooth",
    )(jnp.asarray(rows_mat), jnp.asarray(col_filter(sigma, HALO)), mine, other)


def solution(mesh):
    placed = (
        P(("groups", "patch", "visit"), None, None),
        P(("groups", "patch", "visit")),
        P(("groups", "patch", "visit"), None),
        P(("groups", "patch", "visit"), None),
        P(("groups", "patch", "visit")),
    )

    return jax.shard_map(
        shards,
        mesh=mesh,
        in_specs=placed,
        out_specs=(P(("groups", "patch"), None), P(("groups", "patch"), None)),
        check_vma=False,
    )
```

```python
import functools
import math

import jax
import jax.numpy as jnp
import numpy as np
from jax import lax
from jax.experimental import pallas as pl
from jax.experimental.pallas import tpu as pltpu
from jax.sharding import PartitionSpec as P


BF16, F32, I32 = jnp.bfloat16, jnp.float32, jnp.int32
HALO = 8
PSF_SIGMAS = (0.75, 1.5, 3.0)
PSF_REACH = 16
BASES = len(PSF_SIGMAS)
LANES = 128
WIDE = 2 * LANES
GROUP = 4
PSF_BATCH = 4
DEFERRED = 16
STEPS = 64
OFFSET_MAX = 128
WEIGHT_BITS = 10
WARP_SEGMENT, WARP_EDGE = 32, 8
PSF_SEGMENT, PSF_EDGE = 64, 16


def gaussian(distance, sigma, reach):
    shape = np.exp(-distance * distance / (2.0 * sigma * sigma)) / (math.pi * sigma * sigma) ** 0.25
    return np.where(np.abs(distance) <= reach, shape, 0.0)


def to_bf16(value):
    return value.astype(np.float32).astype(BF16)


def row_filters(rows):
    index = np.arange(rows, dtype=np.float64)
    offset = index[:, None] - index[None, :]
    stacked = np.concatenate([gaussian(offset, s, PSF_REACH) for s in PSF_SIGMAS], axis=0)
    high = to_bf16(stacked)
    return np.concatenate([high, to_bf16(stacked - high.astype(np.float64))], axis=1)


def psf_col_filters():
    lane = np.arange(WIDE, dtype=np.float64)
    offset = lane[None, :] - lane[:, None]
    same = (lane[None, :] // PSF_SEGMENT) == (lane[:, None] // PSF_SEGMENT)
    bands = [gaussian(offset, s, PSF_REACH) for s in PSF_SIGMAS]
    main = np.concatenate(bands, axis=0)
    edge = np.concatenate([np.where(same, band, 0.0) for band in bands], axis=0)
    return to_bf16(main), to_bf16(edge)


def col_filter(sigma, reach):
    lane = np.arange(LANES, dtype=np.float64)
    offset = lane[None, :] - lane[:, None]
    wrapped = (offset + LANES // 2) % LANES - LANES // 2
    circulant = gaussian(wrapped, sigma, reach)
    own = np.where(np.abs(offset) < LANES // 2, circulant, 0.0)
    edge = np.where(np.abs(offset) >= LANES // 2, circulant, 0.0)
    return to_bf16(np.concatenate([own, edge], axis=0))


def lanczos_lines():
    lane = np.arange(LANES, dtype=np.float64)
    wrapped = (lane + LANES // 2) % LANES - LANES // 2
    offset = np.arange(-OFFSET_MAX, OFFSET_MAX + 8, dtype=np.float64)[:, None] / STEPS
    value = wrapped[None, :] + offset
    line = np.where(np.abs(value) < 3.0, np.sinc(value) * np.sinc(value / 3.0), 0.0)
    return line.astype(np.float32)


def digit_bits(devices):
    return max(1, int(math.log2(256 // devices)) if devices <= 128 else 1)


def power_of_two(exponent):
    out = 1.0
    for i in range(6):
        out = out * jnp.where((exponent >> i) & 1 == 1, 2.0 ** (2**i), 1.0)
    return out


def windows(blocks):
    rows = blocks[0].shape[0]
    left = lax.broadcasted_iota(I32, (rows, LANES), 1) < LANES // 2
    zero = jnp.zeros_like(blocks[0])
    padded = [zero, *blocks, zero]
    return jnp.concatenate(
        [
            jnp.concatenate([padded[b + 1], jnp.where(left, padded[b + 2], padded[b])], axis=1)
            for b in range(len(blocks))
        ],
        axis=0,
    )


def block(value, b):
    return value[:, b * LANES : (b + 1) * LANES]


def border_columns(value, segment):
    rows, cols = value.shape
    lane = lax.broadcasted_iota(I32, (rows, LANES), 1)
    per = LANES // segment
    borders = cols // WIDE - 1
    out = []
    for start in range(0, borders, per):
        merged = None
        for s in range(start, min(start + per, borders)):
            both = jnp.where(lane < LANES // 2, block(value, 2 * s + 2), block(value, 2 * s + 1))
            moved = pltpu.roll(both, segment // 2 + segment * (s - start), 1)
            merged = moved if merged is None else jnp.where(lane >= segment * (s - start), moved, merged)
        out.append(merged)
    return out


def mend_borders(blocks, edges, segment, reach):
    rows = blocks[0].shape[0]
    lane = lax.broadcasted_iota(I32, (rows, LANES), 1)
    per = LANES // segment
    blocks = list(blocks)
    for s in range(len(blocks) // 2 - 1):
        shift = LANES - segment // 2 - segment * (s % per)
        moved = pltpu.roll(edges[s // per], shift, 1)
        blocks[2 * s + 1] = jnp.where(lane >= LANES - reach, moved, blocks[2 * s + 1])
        blocks[2 * s + 2] = jnp.where(lane < reach, moved, blocks[2 * s + 2])
    return blocks


def side_by_side(value):
    return jnp.concatenate(
        [value[:, s : s + WIDE] for s in range(0, value.shape[1], WIDE)], axis=0
    )


def stack_kernel(
    bits,
    tile_patch_in,
    raw_weights_in,
    offsets_in,
    coefs_in,
    tiles,
    lines_in,
    row_mats_in,
    col_main_in,
    col_edge_in,
    first_send,
    rest_send,
    first_keep,
    rest_keep,
    raw,
    shifted,
    mixers,
    total,
    stacked,
    strip,
    sems,
    tile_patch,
    raw_weights,
    offsets,
    coefs,
    lines,
    row_mats,
    col_main,
    col_edge,
    in_sems,
    weight_line,
    weight_sem,
    weights,
    patch_line,
    order,
    cursor,
):
    me = lax.axis_index("patch")
    helper = lax.axis_index("visit")
    count, rows, cols = tiles.shape
    patches = cursor.shape[0]
    deferred = stacked.shape[0] == patches
    blocks = cols // LANES
    stripes = rows // 8
    near = (stripes + 2) // 2

    moves = [
        pltpu.make_async_copy(source, target, in_sems.at[i])
        for i, (source, target) in enumerate(
            (
                (tile_patch_in, tile_patch),
                (raw_weights_in, raw_weights),
                (tile_patch_in, patch_line),
                (offsets_in, offsets),
                (coefs_in, coefs),
                (lines_in, lines),
                (row_mats_in, row_mats),
                (col_main_in, col_main),
                (col_edge_in, col_edge),
            )
        )
    ]
    for move in moves:
        move.start()
    for k in range(patches):
        cursor[k] = 0
    moves[0].wait()
    for t in range(count):
        cursor[tile_patch[t]] += 1
    running = 0
    for k in range(patches):
        number = cursor[k]
        cursor[k] = running
        running = running + number
    for t in range(count):
        key = tile_patch[t]
        slot = cursor[key]
        cursor[key] = slot + 1
        order[slot] = t

    groups = -(-count // GROUP)

    def tile_at(g, j):
        return order[jnp.minimum(g * GROUP + j, count - 1)]

    def key_at(g, j):
        slot = g * GROUP + j
        key = tile_patch[order[jnp.minimum(slot, count - 1)]]
        return key if count % GROUP == 0 else jnp.where(slot < count, key, -1)

    def fetch(g, carry):
        for j in range(GROUP):
            pltpu.make_async_copy(tiles.at[tile_at(g, j)], raw.at[g, j], sems.at[g]).start()
        return carry

    lax.fori_loop(0, groups, fetch, 0)

    moves[1].wait()
    weight_line[...] = raw_weights[...].astype(F32)
    weight_copy = pltpu.make_async_copy(weight_line, weights, weight_sem)
    weight_copy.start()
    strip[:blocks] = jnp.zeros((blocks, 8, LANES), F32)
    strip[strip.shape[0] - blocks :] = jnp.zeros((blocks, 8, LANES), F32)
    weight_copy.wait()

    square = lax.broadcasted_iota(I32, (LANES, LANES), 1) - lax.broadcasted_iota(I32, (LANES, LANES), 0)
    ahead, behind = square <= -LANES // 2, square >= LANES // 2
    inner = jnp.abs(square) < LANES // 2
    segment_of = lambda axis: lax.broadcasted_iota(I32, (LANES, LANES), axis) // WARP_SEGMENT
    same_segment = segment_of(0) == segment_of(1)
    half_lanes = lax.broadcasted_iota(I32, (rows, LANES), 1) < LANES // 2
    half_row = lax.broadcasted_iota(I32, (1, LANES), 1) < LANES // 2

    def band(line, height):
        spread = jnp.broadcast_to(line, (height, LANES))
        return pltpu.roll(spread, 0, 1, stride=1, stride_axis=0)

    def line_of(offset):
        return lines[pl.ds(jnp.clip(offset + OFFSET_MAX, 0, 2 * OFFSET_MAX), 1), :]

    def arrive(g):
        pltpu.make_async_copy(tiles.at[pl.ds(0, GROUP)], raw.at[g], sems.at[g]).wait()

    def warp(g):
        slot = g & 1
        ids = [tile_at(g, j) for j in range(GROUP)]
        for j in range(0, GROUP, 2):
            spreads, ends, end_mats = [], [], []
            for i in range(2):
                circulant = band(line_of(offsets[1, ids[j + i]]), LANES)
                pick = lambda mask: jnp.where(mask, circulant, 0.0).astype(BF16)
                own = pick(inner)
                spreads.append(
                    jnp.concatenate(
                        [
                            jnp.concatenate([own, pick(ahead)], axis=1),
                            jnp.concatenate([pick(behind), own], axis=1),
                        ],
                        axis=0,
                    )
                )
                ends.append(border_columns(raw[g, j + i], WARP_SEGMENT)[0])
                end_mats.append(pick(same_segment))
            empty = jnp.zeros((LANES, LANES), BF16)
            mats = jnp.concatenate(
                [
                    jnp.concatenate([end_mats[0], empty], axis=1),
                    jnp.concatenate([empty, end_mats[1]], axis=1),
                ],
                axis=0,
            )
            mended = jnp.dot(
                jnp.concatenate(ends, axis=1), mats, preferred_element_type=F32
            ).astype(BF16)
            for i in range(2):
                value = jnp.dot(
                    side_by_side(raw[g, j + i]), spreads[i], preferred_element_type=F32
                ).astype(BF16)
                blocks = [
                    block(value[s * rows : (s + 1) * rows], b) for s in range(cols // WIDE) for b in range(2)
                ]
                blocks = mend_borders(blocks, [block(mended, i)], WARP_SEGMENT, WARP_EDGE)
                for b, piece in enumerate(blocks):
                    shifted[slot, (j + i) * rows : (j + i + 1) * rows, b * LANES : (b + 1) * LANES] = piece
        pairs = []
        for j in range(0, GROUP, 2):
            one = band(line_of(-offsets[0, ids[j]]), rows)
            two = band(pltpu.roll(line_of(-offsets[0, ids[j + 1]]), LANES // 2, 1), rows)
            pairs.append(jnp.where(half_lanes, one, two).astype(BF16))
        mixer = jnp.concatenate(pairs, axis=1)
        mixer = jnp.concatenate([mixer, mixer], axis=0)
        mixer = jnp.dot(row_mats[...], mixer, preferred_element_type=F32)
        for k in range(BASES):
            scales = [weights[t] * (coefs[k, t].astype(F32) / STEPS) for t in ids]
            scale = jnp.concatenate(
                [jnp.where(half_row, scales[j], scales[j + 1]) for j in range(0, GROUP, 2)], axis=1
            )
            mixers[slot, k * rows : (k + 1) * rows, :] = (mixer[k * rows : (k + 1) * rows] * scale).astype(BF16)

    def group_sum(g, key):
        slot = g & 1
        owner = jnp.concatenate(
            [jnp.where(half_row, key_at(g, j), key_at(g, j + 1)) for j in range(0, GROUP, 2)], axis=1
        )
        mixer = jnp.where(owner == key, mixers[slot], jnp.zeros((), BF16))
        return jnp.dot(mixer, shifted[slot], preferred_element_type=F32)

    def match(q):
        mains, edges = [], []
        for k in range(BASES):
            base_k = stacked[q if deferred else 0, k * rows : (k + 1) * rows, :]
            mains.append(side_by_side(base_k))
            edges.extend(border_columns(base_k, PSF_SEGMENT))
        edge = jnp.dot(jnp.concatenate(edges, axis=1), col_edge[...], preferred_element_type=F32)
        main = jnp.dot(jnp.concatenate(mains, axis=1), col_main[...], preferred_element_type=F32)
        pieces = [block(main[s * rows : (s + 1) * rows], b) for s in range(cols // WIDE) for b in range(2)]
        pieces = mend_borders(pieces, [block(edge, 0), block(edge, 1)], PSF_SEGMENT, PSF_EDGE)
        for b, piece in enumerate(pieces):
            for i in range(stripes):
                strip[(q * stripes + i + 1) * blocks + b] = piece[8 * i : 8 * i + 8]

    def close(g, key, key_end):
        def one(k, carry):
            if deferred:
                stacked[k] = total[...].astype(BF16)
            else:
                stacked[0] = total[...].astype(BF16)
                match(k)
            goes_on = cursor[k] < jnp.minimum((g + 1) * GROUP, count)

            @pl.when(goes_on)
            def _():
                total[...] = group_sum(g, k + 1)

            @pl.when(jnp.logical_not(goes_on))
            def _():
                total[...] = jnp.zeros_like(total)

            return carry

        lax.fori_loop(key, key_end, one, 0)

    for move in moves[2:]:
        move.wait()
    total[...] = jnp.zeros_like(total)
    arrive(0)
    warp(0)

    def step(g, key):
        arrive(g)
        total[...] += group_sum(g - 1, key)
        warp(g)
        key_end = key_at(g, 0)
        close(g - 1, key, key_end)
        return key_end

    key = lax.fori_loop(1, groups, step, jnp.int32(0))
    total[...] += group_sum(groups - 1, key)
    close(groups - 1, key, patches)

    batch = math.gcd(patches, PSF_BATCH)

    def match_some(i, carry):
        for j in range(batch):
            match(i * batch + j)
        return carry

    if deferred:
        lax.fori_loop(0, patches // batch, match_some, 0)

    pairs = patches // 2
    early = first_send.shape[0]
    tile_row = lax.broadcasted_iota(I32, (8, LANES), 0)
    tile_lane = lax.broadcasted_iota(I32, (8, LANES), 1)
    digit_live = tile_lane * bits < WEIGHT_BITS + 30
    scale_up = jnp.where(digit_live, power_of_two((tile_lane + 1) * bits) * 2.0**-WEIGHT_BITS, 0.0)
    line = patch_line[...].reshape(1, count)
    squares = weight_line[...].reshape(1, count)
    squares = squares * squares

    def weight_digits(q, side):
        patch = jnp.where(tile_row[:, :1] == 0, q, q + side)
        mine = (line == patch) & (tile_row[:, :1] < 2)
        scaled = jnp.floor(jnp.sum(jnp.where(mine, squares, 0.0), axis=1, keepdims=True) * scale_up)
        return scaled - 2.0**bits * jnp.floor(scaled * 2.0**-bits)

    def hand_out(start, send, keep):
        def one(i, carry):
            d = start + i
            q = me ^ (2 * ((d + pairs // 2) % pairs) + jnp.where(d < pairs, 1, 0))
            body = near * blocks
            own = pl.ds((q * stripes + helper * near) * blocks, body)
            other = pl.ds((q * stripes + (1 - helper) * near) * blocks, body)
            send[i, :body] = strip[other].astype(BF16)
            send[i, body] = weight_digits(q, 1 - 2 * helper).astype(BF16)
            keep[i, :body] = strip[own]
            keep[i, body] = weight_digits(q, 2 * helper - 1)
            return carry

        lax.fori_loop(0, send.shape[0], one, 0)

    hand_out(0, first_send, first_keep)
    hand_out(early, rest_send, rest_keep)


def message_tiles(rows, cols):
    return (rows // 8 + 2) // 2 * (cols // LANES) + 1


def local_stacks(patches, bits, tile_patch, weights, offsets, coefs, tiles, mats):
    count, rows, cols = tiles.shape
    blocks = cols // LANES
    message = message_tiles(rows, cols)
    groups = -(-count // GROUP)
    hbm = pl.BlockSpec(memory_space=pltpu.HBM)
    return pl.pallas_call(
        functools.partial(stack_kernel, bits),
        out_shape=tuple(
            jax.ShapeDtypeStruct((number, message, 8, LANES), kind)
            for kind in (BF16, F32)
            for number in (patches // 4, patches - patches // 4)
        ),
        in_specs=[hbm] * (5 + len(mats)),
        out_specs=(pl.BlockSpec(memory_space=pltpu.VMEM),) * 4,
        scratch_shapes=[
            pltpu.VMEM((groups, GROUP, rows, cols), BF16),
            pltpu.VMEM((2, GROUP * rows, cols), BF16),
            pltpu.VMEM((2, BASES * rows, GROUP * rows), BF16),
            pltpu.VMEM((BASES * rows, cols), F32),
            pltpu.VMEM((patches if patches <= DEFERRED else 1, BASES * rows, cols), BF16),
            pltpu.VMEM(((patches * rows // 8 + 2) * blocks, 8, LANES), F32),
            pltpu.SemaphoreType.DMA((groups,)),
            pltpu.SMEM((count,), I32),
            pltpu.VMEM((count,), BF16),
            pltpu.SMEM(offsets.shape, I32),
            pltpu.SMEM(coefs.shape, I32),
            *(pltpu.VMEM(m.shape, m.dtype) for m in mats),
            pltpu.SemaphoreType.DMA((5 + len(mats),)),
            pltpu.VMEM((count,), F32),
            pltpu.SemaphoreType.DMA(()),
            pltpu.SMEM((count,), F32),
            pltpu.VMEM((count,), I32),
            pltpu.SMEM((count,), I32),
            pltpu.SMEM((patches,), I32),
        ],
        cost_estimate=pl.CostEstimate(
            flops=2 * count * rows * cols * 4 * WIDE, bytes_accessed=count * rows * cols, transcendentals=0
        ),
        compiler_params=pltpu.CompilerParams(vmem_limit_bytes=48 << 20),
        name="stacks",
    )(*(pltpu.with_memory_space_constraint(a, pltpu.HBM) for a in (tile_patch, weights, offsets, coefs, tiles, *mats)))


def add_kernel(keep, got, *outs):
    start = 0
    for out in outs:
        at = slice(start, start + out.shape[0])
        out[...] = (keep[at] + got[at].astype(F32)).astype(BF16)
        start += out.shape[0]


def merge_kernel(bits, *refs):
    mine = refs[-1]
    near, cols = mine.shape
    blocks = cols // LANES
    total = refs[0][...]
    for got in refs[1:-1]:
        total = total + got[...].astype(F32)
    lane = lax.broadcasted_iota(I32, (8, LANES), 1)
    live = lane * bits < WEIGHT_BITS + 30
    value = jnp.where(live, 2.0**WEIGHT_BITS / power_of_two((lane + 1) * bits), 0.0)
    weight = jnp.sum(total[-1] * value, axis=1, keepdims=True)
    scale = jnp.where(weight > 0.0, 1.0 / jnp.sqrt(jnp.where(weight > 0.0, weight, 1.0)), 0.0)
    inner, outer = scale[0:1], scale[1:2]
    upper = lax.axis_index("visit") == 0
    for i in range(near // 8):
        here = inner
        if i == 0:
            here = jnp.where(upper, outer, inner)
        elif i == near // 8 - 1:
            here = jnp.where(upper, inner, outer)
        for b in range(blocks):
            mine[8 * i : 8 * i + 8, b * LANES : (b + 1) * LANES] = total[i * blocks + b] * here


def smooth_kernel(rows_mat, cols_mat, mine, other, coadd, detection):
    near, cols = mine.shape
    rows = coadd.shape[0]
    upper = lax.axis_index("visit") == 0
    top = jnp.where(upper, mine[...], other[...])
    bottom = jnp.where(upper, other[...], mine[...])
    coadd[: near - HALO, :] = top[HALO:]
    coadd[near - HALO :, :] = bottom[: near - HALO]
    extended = jnp.concatenate([top, bottom], axis=0).astype(BF16)
    blurred = jnp.dot(rows_mat[...], extended, preferred_element_type=F32).astype(BF16)
    blocks = cols // LANES
    window = windows([block(blurred, b) for b in range(blocks)])
    result = jnp.dot(window, cols_mat[...], preferred_element_type=F32)
    for b in range(blocks):
        detection[:, b * LANES : (b + 1) * LANES] = result[b * rows : (b + 1) * rows]


def shards(visit_tiles, tile_patch, offsets, psf_coefs, weights):
    rows, cols = visit_tiles.shape[1:]
    owners = lax.axis_size("patch")
    near = (rows + 2 * HALO) // 2
    bits = digit_bits(owners * lax.axis_size("visit"))
    mats = [jnp.asarray(m) for m in (lanczos_lines(), row_filters(rows), *psf_col_filters())]
    first_send, rest_send, first_keep, rest_keep = local_stacks(
        owners, bits, tile_patch, weights, offsets.T, psf_coefs.T, visit_tiles, mats
    )
    swap = [(0, 1), (1, 0)]
    beside = [(i, i ^ 1) for i in range(owners)]
    pairs = owners // 2
    cut = pairs // 2
    bounds = sorted({0, cut // 2, cut, pairs})
    first_got = lax.ppermute(first_send, "visit", swap)
    first_sums = pl.pallas_call(
        add_kernel,
        out_shape=tuple(
            jax.ShapeDtypeStruct((high - low, *first_keep.shape[1:]), BF16)
            for low, high in zip(bounds[:-2], bounds[1:-1], strict=True)
        ),
        compiler_params=pltpu.CompilerParams(vmem_limit_bytes=16 << 20),
        name="add",
    )(first_keep, first_got)
    rest = rest_keep + lax.ppermute(rest_send, "visit", swap).astype(F32)
    evens = rest[pairs - cut :]
    parts = [evens[cut]]
    for c, (low, high) in enumerate(zip(bounds[:-1], bounds[1:], strict=True)):
        crossing = first_sums[c] if high <= cut else rest[low - cut : high - cut].astype(BF16)
        crossed = lax.ppermute(crossing, "patch", beside)
        local = evens[low:high] if c == 0 else lax.optimization_barrier(evens[low:high])
        for i in range(low, high):
            e = (i + cut) % pairs
            if e == 0:
                parts.append(crossed[i - low])
            else:
                hop = [(j, j ^ (2 * e)) for j in range(owners)]
                summed = (local[i - low] + crossed[i - low].astype(F32)).astype(BF16)
                parts.append(lax.ppermute(summed, "patch", hop))
    mine = pl.pallas_call(
        functools.partial(merge_kernel, bits),
        out_shape=jax.ShapeDtypeStruct((near, cols), F32),
        compiler_params=pltpu.CompilerParams(vmem_limit_bytes=16 << 20),
        name="merge",
    )(*parts)
    other = lax.ppermute(mine, "visit", swap)
    sigma = HALO / 4.0
    out_index = np.arange(rows, dtype=np.float64)[:, None]
    in_index = np.arange(rows + 2 * HALO, dtype=np.float64)[None, :]
    rows_mat = to_bf16(gaussian(out_index + HALO - in_index, sigma, HALO))
    return pl.pallas_call(
        smooth_kernel,
        out_shape=(jax.ShapeDtypeStruct((rows, cols), F32),) * 2,
        compiler_params=pltpu.CompilerParams(vmem_limit_bytes=8 << 20),
        name="smooth",
    )(jnp.asarray(rows_mat), jnp.asarray(col_filter(sigma, HALO)), mine, other)


def solution(mesh):
    placed = (
        P(("groups", "patch", "visit"), None, None),
        P(("groups", "patch", "visit")),
        P(("groups", "patch", "visit"), None),
        P(("groups", "patch", "visit"), None),
        P(("groups", "patch", "visit")),
    )

    return jax.shard_map(
        shards,
        mesh=mesh,
        in_specs=placed,
        out_specs=(P(("groups", "patch"), None), P(("groups", "patch"), None)),
        check_vma=False,
    )
```

```python
import functools
import math

import jax
import jax.numpy as jnp
import numpy as np
from jax import lax
from jax.experimental import pallas as pl
from jax.experimental.pallas import tpu as pltpu
from jax.sharding import PartitionSpec as P


BF16, F32, I32 = jnp.bfloat16, jnp.float32, jnp.int32
HALO = 8
PSF_SIGMAS = (0.75, 1.5, 3.0)
PSF_REACH = 16
BASES = len(PSF_SIGMAS)
LANES = 128
WIDE = 2 * LANES
GROUP = 4
PSF_BATCH = 4
DEFERRED = 16
STEPS = 64
OFFSET_MAX = 128
WEIGHT_BITS = 10
WARP_SEGMENT, WARP_EDGE = 32, 8
PSF_SEGMENT, PSF_EDGE = 64, 16


def gaussian(distance, sigma, reach):
    shape = np.exp(-distance * distance / (2.0 * sigma * sigma)) / (math.pi * sigma * sigma) ** 0.25
    return np.where(np.abs(distance) <= reach, shape, 0.0)


def to_bf16(value):
    return value.astype(np.float32).astype(BF16)


def row_filters(rows):
    index = np.arange(rows, dtype=np.float64)
    offset = index[:, None] - index[None, :]
    stacked = np.concatenate([gaussian(offset, s, PSF_REACH) for s in PSF_SIGMAS], axis=0)
    high = to_bf16(stacked)
    return np.concatenate([high, to_bf16(stacked - high.astype(np.float64))], axis=1)


def psf_col_filters():
    lane = np.arange(WIDE, dtype=np.float64)
    offset = lane[None, :] - lane[:, None]
    same = (lane[None, :] // PSF_SEGMENT) == (lane[:, None] // PSF_SEGMENT)
    bands = [gaussian(offset, s, PSF_REACH) for s in PSF_SIGMAS]
    main = np.concatenate(bands, axis=0)
    edge = np.concatenate([np.where(same, band, 0.0) for band in bands], axis=0)
    return to_bf16(main), to_bf16(edge)


def col_filter(sigma, reach):
    lane = np.arange(LANES, dtype=np.float64)
    offset = lane[None, :] - lane[:, None]
    wrapped = (offset + LANES // 2) % LANES - LANES // 2
    circulant = gaussian(wrapped, sigma, reach)
    own = np.where(np.abs(offset) < LANES // 2, circulant, 0.0)
    edge = np.where(np.abs(offset) >= LANES // 2, circulant, 0.0)
    return to_bf16(np.concatenate([own, edge], axis=0))


def lanczos_lines():
    lane = np.arange(LANES, dtype=np.float64)
    wrapped = (lane + LANES // 2) % LANES - LANES // 2
    offset = np.arange(-OFFSET_MAX, OFFSET_MAX + 8, dtype=np.float64)[:, None] / STEPS
    value = wrapped[None, :] + offset
    line = np.where(np.abs(value) < 3.0, np.sinc(value) * np.sinc(value / 3.0), 0.0)
    return line.astype(np.float32)


def digit_bits(devices):
    return max(1, int(math.log2(256 // devices)) if devices <= 128 else 1)


def power_of_two(exponent):
    out = 1.0
    for i in range(6):
        out = out * jnp.where((exponent >> i) & 1 == 1, 2.0 ** (2**i), 1.0)
    return out


def windows(blocks):
    rows = blocks[0].shape[0]
    left = lax.broadcasted_iota(I32, (rows, LANES), 1) < LANES // 2
    zero = jnp.zeros_like(blocks[0])
    padded = [zero, *blocks, zero]
    return jnp.concatenate(
        [
            jnp.concatenate([padded[b + 1], jnp.where(left, padded[b + 2], padded[b])], axis=1)
            for b in range(len(blocks))
        ],
        axis=0,
    )


def block(value, b):
    return value[:, b * LANES : (b + 1) * LANES]


def border_columns(value, segment):
    rows, cols = value.shape
    lane = lax.broadcasted_iota(I32, (rows, LANES), 1)
    per = LANES // segment
    borders = cols // WIDE - 1
    out = []
    for start in range(0, borders, per):
        merged = None
        for s in range(start, min(start + per, borders)):
            both = jnp.where(lane < LANES // 2, block(value, 2 * s + 2), block(value, 2 * s + 1))
            moved = pltpu.roll(both, segment // 2 + segment * (s - start), 1)
            merged = moved if merged is None else jnp.where(lane >= segment * (s - start), moved, merged)
        out.append(merged)
    return out


def mend_borders(blocks, edges, segment, reach):
    rows = blocks[0].shape[0]
    lane = lax.broadcasted_iota(I32, (rows, LANES), 1)
    per = LANES // segment
    blocks = list(blocks)
    for s in range(len(blocks) // 2 - 1):
        shift = LANES - segment // 2 - segment * (s % per)
        moved = pltpu.roll(edges[s // per], shift, 1)
        blocks[2 * s + 1] = jnp.where(lane >= LANES - reach, moved, blocks[2 * s + 1])
        blocks[2 * s + 2] = jnp.where(lane < reach, moved, blocks[2 * s + 2])
    return blocks


def side_by_side(value):
    return jnp.concatenate(
        [value[:, s : s + WIDE] for s in range(0, value.shape[1], WIDE)], axis=0
    )


def stack_kernel(
    bits,
    tile_patch_in,
    raw_weights_in,
    offsets_in,
    coefs_in,
    tiles,
    lines_in,
    row_mats_in,
    col_main_in,
    col_edge_in,
    first_send,
    rest_send,
    first_keep,
    rest_keep,
    raw,
    shifted,
    mixers,
    total,
    stacked,
    strip,
    sems,
    tile_patch,
    raw_weights,
    offsets,
    coefs,
    lines,
    row_mats,
    col_main,
    col_edge,
    in_sems,
    weight_line,
    weight_sem,
    weights,
    patch_line,
    order,
    cursor,
):
    me = lax.axis_index("patch")
    helper = lax.axis_index("visit")
    count, rows, cols = tiles.shape
    patches = cursor.shape[0]
    deferred = total.shape[0] == patches
    blocks = cols // LANES
    stripes = rows // 8
    near = (stripes + 2) // 2

    moves = [
        pltpu.make_async_copy(source, target, in_sems.at[i])
        for i, (source, target) in enumerate(
            (
                (tile_patch_in, tile_patch),
                (raw_weights_in, raw_weights),
                (tile_patch_in, patch_line),
                (offsets_in, offsets),
                (coefs_in, coefs),
                (lines_in, lines),
                (row_mats_in, row_mats),
                (col_main_in, col_main),
                (col_edge_in, col_edge),
            )
        )
    ]
    for move in moves:
        move.start()
    for k in range(patches):
        cursor[k] = 0
    moves[0].wait()
    for t in range(count):
        cursor[tile_patch[t]] += 1
    running = 0
    for k in range(patches):
        number = cursor[k]
        cursor[k] = running
        running = running + number
    for t in range(count):
        key = tile_patch[t]
        slot = cursor[key]
        cursor[key] = slot + 1
        order[slot] = t

    groups = raw.shape[0]

    def tile_at(g, j):
        return order[jnp.minimum(g * GROUP + j, count - 1)]

    def key_at(g, j):
        slot = g * GROUP + j
        key = tile_patch[order[jnp.minimum(slot, count - 1)]]
        return key if count == groups * GROUP else jnp.where(slot < count, key, -1)

    def real_key(g, j):
        return tile_patch[order[jnp.minimum(g * GROUP + j, count - 1)]]

    def fetch(g, carry):
        for j in range(GROUP):
            pltpu.make_async_copy(tiles.at[tile_at(g, j)], raw.at[g, j], sems.at[g]).start()
        return carry

    lax.fori_loop(0, groups, fetch, 0)

    moves[1].wait()
    weight_line[...] = raw_weights[...].astype(F32)
    weight_copy = pltpu.make_async_copy(weight_line, weights, weight_sem)
    weight_copy.start()
    strip[:blocks] = jnp.zeros((blocks, 8, LANES), F32)
    strip[strip.shape[0] - blocks :] = jnp.zeros((blocks, 8, LANES), F32)
    weight_copy.wait()

    square = lax.broadcasted_iota(I32, (LANES, LANES), 1) - lax.broadcasted_iota(I32, (LANES, LANES), 0)
    ahead, behind = square <= -LANES // 2, square >= LANES // 2
    inner = jnp.abs(square) < LANES // 2
    segment_of = lambda axis: lax.broadcasted_iota(I32, (LANES, LANES), axis) // WARP_SEGMENT
    same_segment = segment_of(0) == segment_of(1)
    half_lanes = lax.broadcasted_iota(I32, (rows, LANES), 1) < LANES // 2
    half_row = lax.broadcasted_iota(I32, (1, LANES), 1) < LANES // 2

    def band(line, height):
        spread = jnp.broadcast_to(line, (height, LANES))
        return pltpu.roll(spread, 0, 1, stride=1, stride_axis=0)

    def line_of(offset):
        return lines[pl.ds(jnp.clip(offset + OFFSET_MAX, 0, 2 * OFFSET_MAX), 1), :]

    def arrive(g):
        pltpu.make_async_copy(tiles.at[pl.ds(0, GROUP)], raw.at[g], sems.at[g]).wait()

    def warp(g):
        slot = g & (shifted.shape[0] - 1)
        ids = [tile_at(g, j) for j in range(GROUP)]
        for j in range(0, GROUP, 2):
            spreads, ends, end_mats = [], [], []
            for i in range(2):
                circulant = band(line_of(offsets[1, ids[j + i]]), LANES)
                pick = lambda mask: jnp.where(mask, circulant, 0.0).astype(BF16)
                own = pick(inner)
                spreads.append(
                    jnp.concatenate(
                        [
                            jnp.concatenate([own, pick(ahead)], axis=1),
                            jnp.concatenate([pick(behind), own], axis=1),
                        ],
                        axis=0,
                    )
                )
                ends.append(border_columns(raw[g, j + i], WARP_SEGMENT)[0])
                end_mats.append(pick(same_segment))
            empty = jnp.zeros((LANES, LANES), BF16)
            mats = jnp.concatenate(
                [
                    jnp.concatenate([end_mats[0], empty], axis=1),
                    jnp.concatenate([empty, end_mats[1]], axis=1),
                ],
                axis=0,
            )
            mended = jnp.dot(
                jnp.concatenate(ends, axis=1), mats, preferred_element_type=F32
            ).astype(BF16)
            for i in range(2):
                value = jnp.dot(
                    side_by_side(raw[g, j + i]), spreads[i], preferred_element_type=F32
                ).astype(BF16)
                blocks = [
                    block(value[s * rows : (s + 1) * rows], b) for s in range(cols // WIDE) for b in range(2)
                ]
                blocks = mend_borders(blocks, [block(mended, i)], WARP_SEGMENT, WARP_EDGE)
                for b, piece in enumerate(blocks):
                    shifted[slot, (j + i) * rows : (j + i + 1) * rows, b * LANES : (b + 1) * LANES] = piece
        pairs = []
        for j in range(0, GROUP, 2):
            one = band(line_of(-offsets[0, ids[j]]), rows)
            two = band(pltpu.roll(line_of(-offsets[0, ids[j + 1]]), LANES // 2, 1), rows)
            pairs.append(jnp.where(half_lanes, one, two).astype(BF16))
        mixer = jnp.concatenate(pairs, axis=1)
        mixer = jnp.concatenate([mixer, mixer], axis=0)
        mixer = jnp.dot(row_mats[...], mixer, preferred_element_type=F32)
        for k in range(BASES):
            scales = [weights[t] * (coefs[k, t].astype(F32) / STEPS) for t in ids]
            scale = jnp.concatenate(
                [jnp.where(half_row, scales[j], scales[j + 1]) for j in range(0, GROUP, 2)], axis=1
            )
            mixers[slot, k * rows : (k + 1) * rows, :] = (mixer[k * rows : (k + 1) * rows] * scale).astype(BF16)

    def group_sum(g, key):
        slot = g & (shifted.shape[0] - 1)
        owner = jnp.concatenate(
            [jnp.where(half_row, key_at(g, j), key_at(g, j + 1)) for j in range(0, GROUP, 2)], axis=1
        )
        mixer = jnp.where(owner == key, mixers[slot], jnp.zeros((), BF16))
        return jnp.dot(mixer, shifted[slot], preferred_element_type=F32)

    def match(q):
        mains, edges = [], []
        for k in range(BASES):
            band_k = slice(k * rows, (k + 1) * rows)
            base_k = total[q, band_k, :].astype(BF16) if deferred else stacked[band_k, :]
            mains.append(side_by_side(base_k))
            edges.extend(border_columns(base_k, PSF_SEGMENT))
        edge = jnp.dot(jnp.concatenate(edges, axis=1), col_edge[...], preferred_element_type=F32)
        main = jnp.dot(jnp.concatenate(mains, axis=1), col_main[...], preferred_element_type=F32)
        pieces = [block(main[s * rows : (s + 1) * rows], b) for s in range(cols // WIDE) for b in range(2)]
        pieces = mend_borders(pieces, [block(edge, 0), block(edge, 1)], PSF_SEGMENT, PSF_EDGE)
        for b, piece in enumerate(pieces):
            for i in range(stripes):
                strip[(q * stripes + i + 1) * blocks + b] = piece[8 * i : 8 * i + 8]

    def close(g, key, key_end):
        def one(k, carry):
            stacked[...] = total[0].astype(BF16)
            match(k)
            total[0] = group_sum(g, k + 1)
            return carry

        lax.fori_loop(key, key_end, one, 0)

    def share(g):
        def one(k, carry):
            total[k] += group_sum(g, k)
            return carry

        lax.fori_loop(real_key(g, 0) + 1, real_key(g, GROUP - 1) + 1, one, 0)

    for move in moves[2:]:
        move.wait()
    total[...] = jnp.zeros_like(total)
    if deferred:
        for g in range(2):
            arrive(g)
        for g in range(2):
            warp(g)

        def step(i, carry):
            g = 2 * i
            for j in range(2):
                arrive(g + j)
            for j in range(2):
                total[real_key(g - 2 + j, 0)] += group_sum(g - 2 + j, real_key(g - 2 + j, 0))
            for j in range(2):
                warp(g + j)
            for j in range(2):
                share(g - 2 + j)
            return carry

        lax.fori_loop(1, groups // 2, step, 0)
        for g in (groups - 2, groups - 1):
            total[real_key(g, 0)] += group_sum(g, real_key(g, 0))
        for g in (groups - 2, groups - 1):
            share(g)
    else:
        arrive(0)
        warp(0)

        def step(g, key):
            arrive(g)
            total[0] += group_sum(g - 1, key)
            warp(g)
            key_end = real_key(g, 0)
            close(g - 1, key, key_end)
            return key_end

        key = lax.fori_loop(1, groups, step, jnp.int32(0))
        total[0] += group_sum(groups - 1, key)
        close(groups - 1, key, patches)

    batch = math.gcd(patches, PSF_BATCH)

    def match_some(i, carry):
        for j in range(batch):
            match(i * batch + j)
        return carry

    if deferred:
        lax.fori_loop(0, patches // batch, match_some, 0)

    pairs = patches // 2
    early = first_send.shape[0]
    tile_row = lax.broadcasted_iota(I32, (8, LANES), 0)
    tile_lane = lax.broadcasted_iota(I32, (8, LANES), 1)
    digit_live = tile_lane * bits < WEIGHT_BITS + 30
    scale_up = jnp.where(digit_live, power_of_two((tile_lane + 1) * bits) * 2.0**-WEIGHT_BITS, 0.0)
    line = patch_line[...].reshape(1, count)
    squares = weight_line[...].reshape(1, count)
    squares = squares * squares

    def weight_digits(q, side):
        patch = jnp.where(tile_row[:, :1] == 0, q, q + side)
        mine = (line == patch) & (tile_row[:, :1] < 2)
        scaled = jnp.floor(jnp.sum(jnp.where(mine, squares, 0.0), axis=1, keepdims=True) * scale_up)
        return scaled - 2.0**bits * jnp.floor(scaled * 2.0**-bits)

    def hand_out(start, send, keep):
        def one(i, carry):
            d = start + i
            q = me ^ (2 * ((d + pairs // 2) % pairs) + jnp.where(d < pairs, 1, 0))
            body = near * blocks
            own = pl.ds((q * stripes + helper * near) * blocks, body)
            other = pl.ds((q * stripes + (1 - helper) * near) * blocks, body)
            send[i, :body] = strip[other].astype(BF16)
            send[i, body] = weight_digits(q, 1 - 2 * helper).astype(BF16)
            keep[i, :body] = strip[own]
            keep[i, body] = weight_digits(q, 2 * helper - 1)
            return carry

        lax.fori_loop(0, send.shape[0], one, 0)

    hand_out(0, first_send, first_keep)
    hand_out(early, rest_send, rest_keep)


def message_tiles(rows, cols):
    return (rows // 8 + 2) // 2 * (cols // LANES) + 1


def local_stacks(patches, bits, tile_patch, weights, offsets, coefs, tiles, mats):
    count, rows, cols = tiles.shape
    blocks = cols // LANES
    message = message_tiles(rows, cols)
    deferred = patches <= DEFERRED
    groups = -(-count // GROUP)
    groups += groups % 2 if deferred else 0
    hbm = pl.BlockSpec(memory_space=pltpu.HBM)
    return pl.pallas_call(
        functools.partial(stack_kernel, bits),
        out_shape=tuple(
            jax.ShapeDtypeStruct((number, message, 8, LANES), kind)
            for kind in (BF16, F32)
            for number in (patches // 4, patches - patches // 4)
        ),
        in_specs=[hbm] * (5 + len(mats)),
        out_specs=(pl.BlockSpec(memory_space=pltpu.VMEM),) * 4,
        scratch_shapes=[
            pltpu.VMEM((groups, GROUP, rows, cols), BF16),
            pltpu.VMEM((4 if deferred else 2, GROUP * rows, cols), BF16),
            pltpu.VMEM((4 if deferred else 2, BASES * rows, GROUP * rows), BF16),
            pltpu.VMEM((patches if deferred else 1, BASES * rows, cols), F32),
            pltpu.VMEM((8 if deferred else BASES * rows, LANES if deferred else cols), BF16),
            pltpu.VMEM(((patches * rows // 8 + 2) * blocks, 8, LANES), F32),
            pltpu.SemaphoreType.DMA((groups,)),
            pltpu.SMEM((count,), I32),
            pltpu.VMEM((count,), BF16),
            pltpu.SMEM(offsets.shape, I32),
            pltpu.SMEM(coefs.shape, I32),
            *(pltpu.VMEM(m.shape, m.dtype) for m in mats),
            pltpu.SemaphoreType.DMA((5 + len(mats),)),
            pltpu.VMEM((count,), F32),
            pltpu.SemaphoreType.DMA(()),
            pltpu.SMEM((count,), F32),
            pltpu.VMEM((count,), I32),
            pltpu.SMEM((count,), I32),
            pltpu.SMEM((patches,), I32),
        ],
        cost_estimate=pl.CostEstimate(
            flops=2 * count * rows * cols * 4 * WIDE, bytes_accessed=count * rows * cols, transcendentals=0
        ),
        compiler_params=pltpu.CompilerParams(vmem_limit_bytes=48 << 20),
        name="stacks",
    )(*(pltpu.with_memory_space_constraint(a, pltpu.HBM) for a in (tile_patch, weights, offsets, coefs, tiles, *mats)))


def add_kernel(keep, got, *outs):
    start = 0
    for out in outs:
        at = slice(start, start + out.shape[0])
        out[...] = (keep[at] + got[at].astype(F32)).astype(BF16)
        start += out.shape[0]


def merge_kernel(bits, *refs):
    mine = refs[-1]
    near, cols = mine.shape
    blocks = cols // LANES
    total = refs[0][...]
    for got in refs[1:-1]:
        total = total + got[...].astype(F32)
    lane = lax.broadcasted_iota(I32, (8, LANES), 1)
    live = lane * bits < WEIGHT_BITS + 30
    value = jnp.where(live, 2.0**WEIGHT_BITS / power_of_two((lane + 1) * bits), 0.0)
    weight = jnp.sum(total[-1] * value, axis=1, keepdims=True)
    scale = jnp.where(weight > 0.0, 1.0 / jnp.sqrt(jnp.where(weight > 0.0, weight, 1.0)), 0.0)
    inner, outer = scale[0:1], scale[1:2]
    upper = lax.axis_index("visit") == 0
    for i in range(near // 8):
        here = inner
        if i == 0:
            here = jnp.where(upper, outer, inner)
        elif i == near // 8 - 1:
            here = jnp.where(upper, inner, outer)
        for b in range(blocks):
            mine[8 * i : 8 * i + 8, b * LANES : (b + 1) * LANES] = total[i * blocks + b] * here


def smooth_kernel(rows_mat, cols_mat, mine, other, coadd, detection):
    near, cols = mine.shape
    rows = coadd.shape[0]
    upper = lax.axis_index("visit") == 0
    top = jnp.where(upper, mine[...], other[...])
    bottom = jnp.where(upper, other[...], mine[...])
    coadd[: near - HALO, :] = top[HALO:]
    coadd[near - HALO :, :] = bottom[: near - HALO]
    extended = jnp.concatenate([top, bottom], axis=0).astype(BF16)
    blurred = jnp.dot(rows_mat[...], extended, preferred_element_type=F32).astype(BF16)
    blocks = cols // LANES
    window = windows([block(blurred, b) for b in range(blocks)])
    result = jnp.dot(window, cols_mat[...], preferred_element_type=F32)
    for b in range(blocks):
        detection[:, b * LANES : (b + 1) * LANES] = result[b * rows : (b + 1) * rows]


def shards(visit_tiles, tile_patch, offsets, psf_coefs, weights):
    rows, cols = visit_tiles.shape[1:]
    owners = lax.axis_size("patch")
    near = (rows + 2 * HALO) // 2
    bits = digit_bits(owners * lax.axis_size("visit"))
    mats = [jnp.asarray(m) for m in (lanczos_lines(), row_filters(rows), *psf_col_filters())]
    first_send, rest_send, first_keep, rest_keep = local_stacks(
        owners, bits, tile_patch, weights, offsets.T, psf_coefs.T, visit_tiles, mats
    )
    swap = [(0, 1), (1, 0)]
    beside = [(i, i ^ 1) for i in range(owners)]
    pairs = owners // 2
    cut = pairs // 2
    bounds = sorted({0, cut // 2, cut, pairs})
    first_got = lax.ppermute(first_send, "visit", swap)
    first_sums = pl.pallas_call(
        add_kernel,
        out_shape=tuple(
            jax.ShapeDtypeStruct((high - low, *first_keep.shape[1:]), BF16)
            for low, high in zip(bounds[:-2], bounds[1:-1], strict=True)
        ),
        compiler_params=pltpu.CompilerParams(vmem_limit_bytes=16 << 20),
        name="add",
    )(first_keep, first_got)
    rest = rest_keep + lax.ppermute(rest_send, "visit", swap).astype(F32)
    evens = rest[pairs - cut :]
    parts = [evens[cut]]
    for c, (low, high) in enumerate(zip(bounds[:-1], bounds[1:], strict=True)):
        crossing = first_sums[c] if high <= cut else rest[low - cut : high - cut].astype(BF16)
        crossed = lax.ppermute(crossing, "patch", beside)
        local = evens[low:high] if c == 0 else lax.optimization_barrier(evens[low:high])
        for i in range(low, high):
            e = (i + cut) % pairs
            if e == 0:
                parts.append(crossed[i - low])
            else:
                hop = [(j, j ^ (2 * e)) for j in range(owners)]
                summed = (local[i - low] + crossed[i - low].astype(F32)).astype(BF16)
                parts.append(lax.ppermute(summed, "patch", hop))
    mine = pl.pallas_call(
        functools.partial(merge_kernel, bits),
        out_shape=jax.ShapeDtypeStruct((near, cols), F32),
        compiler_params=pltpu.CompilerParams(vmem_limit_bytes=16 << 20),
        name="merge",
    )(*parts)
    other = lax.ppermute(mine, "visit", swap)
    sigma = HALO / 4.0
    out_index = np.arange(rows, dtype=np.float64)[:, None]
    in_index = np.arange(rows + 2 * HALO, dtype=np.float64)[None, :]
    rows_mat = to_bf16(gaussian(out_index + HALO - in_index, sigma, HALO))
    return pl.pallas_call(
        smooth_kernel,
        out_shape=(jax.ShapeDtypeStruct((rows, cols), F32),) * 2,
        compiler_params=pltpu.CompilerParams(vmem_limit_bytes=8 << 20),
        name="smooth",
    )(jnp.asarray(rows_mat), jnp.asarray(col_filter(sigma, HALO)), mine, other)


def solution(mesh):
    placed = (
        P(("groups", "patch", "visit"), None, None),
        P(("groups", "patch", "visit")),
        P(("groups", "patch", "visit"), None),
        P(("groups", "patch", "visit"), None),
        P(("groups", "patch", "visit")),
    )

    return jax.shard_map(
        shards,
        mesh=mesh,
        in_specs=placed,
        out_specs=(P(("groups", "patch"), None), P(("groups", "patch"), None)),
        check_vma=False,
    )
```

```python
import functools
import math

import jax
import jax.numpy as jnp
import numpy as np
from jax import lax
from jax.experimental import pallas as pl
from jax.experimental.pallas import tpu as pltpu
from jax.sharding import PartitionSpec as P


BF16, F32, I32 = jnp.bfloat16, jnp.float32, jnp.int32
HALO = 8
PSF_SIGMAS = (0.75, 1.5, 3.0)
PSF_REACH = 16
BASES = len(PSF_SIGMAS)
LANES = 128
WIDE = 2 * LANES
GROUP = 4
PSF_BATCH = 8
DEFERRED = 16
STEPS = 64
OFFSET_MAX = 128
WEIGHT_BITS = 10
WARP_SEGMENT, WARP_EDGE = 32, 8
PSF_SEGMENT, PSF_EDGE = 64, 16


def gaussian(distance, sigma, reach):
    shape = np.exp(-distance * distance / (2.0 * sigma * sigma)) / (math.pi * sigma * sigma) ** 0.25
    return np.where(np.abs(distance) <= reach, shape, 0.0)


def to_bf16(value):
    return value.astype(np.float32).astype(BF16)


def row_filters(rows):
    index = np.arange(rows, dtype=np.float64)
    offset = index[:, None] - index[None, :]
    stacked = np.concatenate([gaussian(offset, s, PSF_REACH) for s in PSF_SIGMAS], axis=0)
    high = to_bf16(stacked)
    return np.concatenate([high, to_bf16(stacked - high.astype(np.float64))], axis=1)


def psf_col_filters():
    lane = np.arange(WIDE, dtype=np.float64)
    offset = lane[None, :] - lane[:, None]
    same = (lane[None, :] // PSF_SEGMENT) == (lane[:, None] // PSF_SEGMENT)
    bands = [gaussian(offset, s, PSF_REACH) for s in PSF_SIGMAS]
    main = np.concatenate(bands, axis=0)
    edge = np.concatenate([np.where(same, band, 0.0) for band in bands], axis=0)
    return to_bf16(main), to_bf16(edge)


def col_filter(sigma, reach):
    lane = np.arange(LANES, dtype=np.float64)
    offset = lane[None, :] - lane[:, None]
    wrapped = (offset + LANES // 2) % LANES - LANES // 2
    circulant = gaussian(wrapped, sigma, reach)
    own = np.where(np.abs(offset) < LANES // 2, circulant, 0.0)
    edge = np.where(np.abs(offset) >= LANES // 2, circulant, 0.0)
    return to_bf16(np.concatenate([own, edge], axis=0))


def lanczos_lines():
    lane = np.arange(LANES, dtype=np.float64)
    wrapped = (lane + LANES // 2) % LANES - LANES // 2
    offset = np.arange(-OFFSET_MAX, OFFSET_MAX + 8, dtype=np.float64)[:, None] / STEPS
    value = wrapped[None, :] + offset
    line = np.where(np.abs(value) < 3.0, np.sinc(value) * np.sinc(value / 3.0), 0.0)
    return line.astype(np.float32)


def digit_bits(devices):
    return max(1, int(math.log2(256 // devices)) if devices <= 128 else 1)


def power_of_two(exponent):
    out = 1.0
    for i in range(6):
        out = out * jnp.where((exponent >> i) & 1 == 1, 2.0 ** (2**i), 1.0)
    return out


def windows(blocks):
    rows = blocks[0].shape[0]
    left = lax.broadcasted_iota(I32, (rows, LANES), 1) < LANES // 2
    zero = jnp.zeros_like(blocks[0])
    padded = [zero, *blocks, zero]
    return jnp.concatenate(
        [
            jnp.concatenate([padded[b + 1], jnp.where(left, padded[b + 2], padded[b])], axis=1)
            for b in range(len(blocks))
        ],
        axis=0,
    )


def block(value, b):
    return value[:, b * LANES : (b + 1) * LANES]


def border_columns(value, segment):
    rows, cols = value.shape
    lane = lax.broadcasted_iota(I32, (rows, LANES), 1)
    per = LANES // segment
    borders = cols // WIDE - 1
    out = []
    for start in range(0, borders, per):
        merged = None
        for s in range(start, min(start + per, borders)):
            both = jnp.where(lane < LANES // 2, block(value, 2 * s + 2), block(value, 2 * s + 1))
            moved = pltpu.roll(both, segment // 2 + segment * (s - start), 1)
            merged = moved if merged is None else jnp.where(lane >= segment * (s - start), moved, merged)
        out.append(merged)
    return out


def mend_borders(blocks, edges, segment, reach):
    rows = blocks[0].shape[0]
    lane = lax.broadcasted_iota(I32, (rows, LANES), 1)
    per = LANES // segment
    blocks = list(blocks)
    for s in range(len(blocks) // 2 - 1):
        shift = LANES - segment // 2 - segment * (s % per)
        moved = pltpu.roll(edges[s // per], shift, 1)
        blocks[2 * s + 1] = jnp.where(lane >= LANES - reach, moved, blocks[2 * s + 1])
        blocks[2 * s + 2] = jnp.where(lane < reach, moved, blocks[2 * s + 2])
    return blocks


def side_by_side(value):
    return jnp.concatenate(
        [value[:, s : s + WIDE] for s in range(0, value.shape[1], WIDE)], axis=0
    )


def stack_kernel(
    bits,
    tile_patch_in,
    raw_weights_in,
    offsets_in,
    coefs_in,
    tiles,
    lines_in,
    row_mats_in,
    col_main_in,
    col_edge_in,
    first_send,
    rest_send,
    first_keep,
    rest_keep,
    raw,
    shifted,
    mixers,
    total,
    stacked,
    strip,
    sems,
    tile_patch,
    raw_weights,
    offsets,
    coefs,
    lines,
    row_mats,
    col_main,
    col_edge,
    in_sems,
    weight_line,
    weight_sem,
    weights,
    patch_line,
    order,
    cursor,
):
    me = lax.axis_index("patch")
    helper = lax.axis_index("visit")
    count, rows, cols = tiles.shape
    patches = cursor.shape[0]
    deferred = total.shape[0] == patches
    blocks = cols // LANES
    stripes = rows // 8
    near = (stripes + 2) // 2

    moves = [
        pltpu.make_async_copy(source, target, in_sems.at[i])
        for i, (source, target) in enumerate(
            (
                (tile_patch_in, tile_patch),
                (raw_weights_in, raw_weights),
                (tile_patch_in, patch_line),
                (offsets_in, offsets),
                (coefs_in, coefs),
                (lines_in, lines),
                (row_mats_in, row_mats),
                (col_main_in, col_main),
                (col_edge_in, col_edge),
            )
        )
    ]
    for move in moves:
        move.start()
    for k in range(patches):
        cursor[k] = 0
    total[...] = jnp.zeros_like(total)
    moves[0].wait()
    for t in range(count):
        cursor[tile_patch[t]] += 1
    running = 0
    for k in range(patches):
        number = cursor[k]
        cursor[k] = running
        running = running + number
    for t in range(count):
        key = tile_patch[t]
        slot = cursor[key]
        cursor[key] = slot + 1
        order[slot] = t

    groups = raw.shape[0]

    def tile_at(g, j):
        return order[jnp.minimum(g * GROUP + j, count - 1)]

    def key_at(g, j):
        slot = g * GROUP + j
        key = tile_patch[order[jnp.minimum(slot, count - 1)]]
        return key if count == groups * GROUP else jnp.where(slot < count, key, -1)

    def real_key(g, j):
        return tile_patch[order[jnp.minimum(g * GROUP + j, count - 1)]]

    def fetch(g, carry):
        for j in range(GROUP):
            pltpu.make_async_copy(tiles.at[tile_at(g, j)], raw.at[g, j], sems.at[g]).start()
        return carry

    lax.fori_loop(0, groups, fetch, 0)

    moves[1].wait()
    weight_line[...] = raw_weights[...].astype(F32)
    weight_copy = pltpu.make_async_copy(weight_line, weights, weight_sem)
    weight_copy.start()
    strip[:blocks] = jnp.zeros((blocks, 8, LANES), F32)
    strip[strip.shape[0] - blocks :] = jnp.zeros((blocks, 8, LANES), F32)
    weight_copy.wait()

    square = lax.broadcasted_iota(I32, (LANES, LANES), 1) - lax.broadcasted_iota(I32, (LANES, LANES), 0)
    ahead, behind = square <= -LANES // 2, square >= LANES // 2
    inner = jnp.abs(square) < LANES // 2
    segment_of = lambda axis: lax.broadcasted_iota(I32, (LANES, LANES), axis) // WARP_SEGMENT
    same_segment = segment_of(0) == segment_of(1)
    half_lanes = lax.broadcasted_iota(I32, (rows, LANES), 1) < LANES // 2
    half_row = lax.broadcasted_iota(I32, (1, LANES), 1) < LANES // 2

    def band(line, height):
        spread = jnp.broadcast_to(line, (height, LANES))
        return pltpu.roll(spread, 0, 1, stride=1, stride_axis=0)

    def line_of(offset):
        return lines[pl.ds(jnp.clip(offset + OFFSET_MAX, 0, 2 * OFFSET_MAX), 1), :]

    def arrive(g):
        pltpu.make_async_copy(tiles.at[pl.ds(0, GROUP)], raw.at[g], sems.at[g]).wait()

    def warp(g):
        slot = g & (shifted.shape[0] - 1)
        ids = [tile_at(g, j) for j in range(GROUP)]
        for j in range(0, GROUP, 2):
            spreads, ends, end_mats = [], [], []
            for i in range(2):
                circulant = band(line_of(offsets[1, ids[j + i]]), LANES)
                pick = lambda mask: jnp.where(mask, circulant, 0.0).astype(BF16)
                own = pick(inner)
                spreads.append(
                    jnp.concatenate(
                        [
                            jnp.concatenate([own, pick(ahead)], axis=1),
                            jnp.concatenate([pick(behind), own], axis=1),
                        ],
                        axis=0,
                    )
                )
                ends.append(border_columns(raw[g, j + i], WARP_SEGMENT)[0])
                end_mats.append(pick(same_segment))
            empty = jnp.zeros((LANES, LANES), BF16)
            mats = jnp.concatenate(
                [
                    jnp.concatenate([end_mats[0], empty], axis=1),
                    jnp.concatenate([empty, end_mats[1]], axis=1),
                ],
                axis=0,
            )
            mended = jnp.dot(
                jnp.concatenate(ends, axis=1), mats, preferred_element_type=F32
            ).astype(BF16)
            for i in range(2):
                value = jnp.dot(
                    side_by_side(raw[g, j + i]), spreads[i], preferred_element_type=F32
                ).astype(BF16)
                blocks = [
                    block(value[s * rows : (s + 1) * rows], b) for s in range(cols // WIDE) for b in range(2)
                ]
                blocks = mend_borders(blocks, [block(mended, i)], WARP_SEGMENT, WARP_EDGE)
                for b, piece in enumerate(blocks):
                    shifted[slot, (j + i) * rows : (j + i + 1) * rows, b * LANES : (b + 1) * LANES] = piece
        pairs = []
        for j in range(0, GROUP, 2):
            one = band(line_of(-offsets[0, ids[j]]), rows)
            two = band(pltpu.roll(line_of(-offsets[0, ids[j + 1]]), LANES // 2, 1), rows)
            pairs.append(jnp.where(half_lanes, one, two).astype(BF16))
        mixer = jnp.concatenate(pairs, axis=1)
        mixer = jnp.concatenate([mixer, mixer], axis=0)
        mixer = jnp.dot(row_mats[...], mixer, preferred_element_type=F32)
        for k in range(BASES):
            scales = [weights[t] * (coefs[k, t].astype(F32) / STEPS) for t in ids]
            scale = jnp.concatenate(
                [jnp.where(half_row, scales[j], scales[j + 1]) for j in range(0, GROUP, 2)], axis=1
            )
            mixers[slot, k * rows : (k + 1) * rows, :] = (mixer[k * rows : (k + 1) * rows] * scale).astype(BF16)

    def group_sum(g, key):
        slot = g & (shifted.shape[0] - 1)
        owner = jnp.concatenate(
            [jnp.where(half_row, key_at(g, j), key_at(g, j + 1)) for j in range(0, GROUP, 2)], axis=1
        )
        mixer = jnp.where(owner == key, mixers[slot], jnp.zeros((), BF16))
        return jnp.dot(mixer, shifted[slot], preferred_element_type=F32)

    def match(q):
        mains, edges = [], []
        for k in range(BASES):
            band_k = slice(k * rows, (k + 1) * rows)
            base_k = total[q, band_k, :].astype(BF16) if deferred else stacked[band_k, :]
            mains.append(side_by_side(base_k))
            edges.extend(border_columns(base_k, PSF_SEGMENT))
        edge = jnp.dot(jnp.concatenate(edges, axis=1), col_edge[...], preferred_element_type=F32)
        main = jnp.dot(jnp.concatenate(mains, axis=1), col_main[...], preferred_element_type=F32)
        pieces = [block(main[s * rows : (s + 1) * rows], b) for s in range(cols // WIDE) for b in range(2)]
        pieces = mend_borders(pieces, [block(edge, 0), block(edge, 1)], PSF_SEGMENT, PSF_EDGE)
        for b, piece in enumerate(pieces):
            for i in range(stripes):
                strip[(q * stripes + i + 1) * blocks + b] = piece[8 * i : 8 * i + 8]

    def close(g, key, key_end):
        def one(k, carry):
            stacked[...] = total[0].astype(BF16)
            match(k)
            total[0] = group_sum(g, k + 1)
            return carry

        lax.fori_loop(key, key_end, one, 0)

    def share(g):
        def one(k, carry):
            total[k] += group_sum(g, k)
            return carry

        lax.fori_loop(real_key(g, 0) + 1, real_key(g, GROUP - 1) + 1, one, 0)

    for move in moves[2:]:
        move.wait()
    if deferred:
        for g in range(2):
            arrive(g)
        for g in range(2):
            warp(g)

        def step(i, carry):
            g = 2 * i
            for j in range(2):
                arrive(g + j)
            for j in range(2):
                total[real_key(g - 2 + j, 0)] += group_sum(g - 2 + j, real_key(g - 2 + j, 0))
            for j in range(2):
                warp(g + j)
            for j in range(2):
                share(g - 2 + j)
            return carry

        lax.fori_loop(1, groups // 2, step, 0)
        for g in (groups - 2, groups - 1):
            total[real_key(g, 0)] += group_sum(g, real_key(g, 0))
        for g in (groups - 2, groups - 1):
            share(g)
    else:
        arrive(0)
        warp(0)

        def step(g, key):
            arrive(g)
            total[0] += group_sum(g - 1, key)
            warp(g)
            key_end = real_key(g, 0)
            close(g - 1, key, key_end)
            return key_end

        key = lax.fori_loop(1, groups, step, jnp.int32(0))
        total[0] += group_sum(groups - 1, key)
        close(groups - 1, key, patches)

    batch = math.gcd(patches, PSF_BATCH)

    def match_some(i, carry):
        for j in range(batch):
            match(i * batch + j)
        return carry

    if deferred:
        lax.fori_loop(0, patches // batch, match_some, 0)

    pairs = patches // 2
    early = first_send.shape[0]
    tile_row = lax.broadcasted_iota(I32, (8, LANES), 0)
    tile_lane = lax.broadcasted_iota(I32, (8, LANES), 1)
    digit_live = tile_lane * bits < WEIGHT_BITS + 30
    scale_up = jnp.where(digit_live, power_of_two((tile_lane + 1) * bits) * 2.0**-WEIGHT_BITS, 0.0)
    line = patch_line[...].reshape(1, count)
    squares = weight_line[...].reshape(1, count)
    squares = squares * squares

    def weight_digits(q, side):
        patch = jnp.where(tile_row[:, :1] == 0, q, q + side)
        mine = (line == patch) & (tile_row[:, :1] < 2)
        scaled = jnp.floor(jnp.sum(jnp.where(mine, squares, 0.0), axis=1, keepdims=True) * scale_up)
        return scaled - 2.0**bits * jnp.floor(scaled * 2.0**-bits)

    def hand_out(start, send, keep):
        def one(i):
            d = start + i
            q = me ^ (2 * ((d + pairs // 2) % pairs) + jnp.where(d < pairs, 1, 0))
            body = near * blocks
            own = pl.ds((q * stripes + helper * near) * blocks, body)
            other = pl.ds((q * stripes + (1 - helper) * near) * blocks, body)
            send[i, :body] = strip[other].astype(BF16)
            send[i, body] = weight_digits(q, 1 - 2 * helper).astype(BF16)
            keep[i, :body] = strip[own]
            keep[i, body] = weight_digits(q, 2 * helper - 1)

        step = math.gcd(send.shape[0], 6)

        def some(i, carry):
            for j in range(step):
                one(i * step + j)
            return carry

        lax.fori_loop(0, send.shape[0] // step, some, 0)

    hand_out(0, first_send, first_keep)
    hand_out(early, rest_send, rest_keep)


def message_tiles(rows, cols):
    return (rows // 8 + 2) // 2 * (cols // LANES) + 1


def local_stacks(patches, bits, tile_patch, weights, offsets, coefs, tiles, mats):
    count, rows, cols = tiles.shape
    blocks = cols // LANES
    message = message_tiles(rows, cols)
    deferred = patches <= DEFERRED
    groups = -(-count // GROUP)
    groups += groups % 2 if deferred else 0
    hbm = pl.BlockSpec(memory_space=pltpu.HBM)
    return pl.pallas_call(
        functools.partial(stack_kernel, bits),
        out_shape=tuple(
            jax.ShapeDtypeStruct((number, message, 8, LANES), kind)
            for kind in (BF16, F32)
            for number in (patches // 4, patches - patches // 4)
        ),
        in_specs=[hbm] * (5 + len(mats)),
        out_specs=(pl.BlockSpec(memory_space=pltpu.VMEM),) * 4,
        scratch_shapes=[
            pltpu.VMEM((groups, GROUP, rows, cols), BF16),
            pltpu.VMEM((4 if deferred else 2, GROUP * rows, cols), BF16),
            pltpu.VMEM((4 if deferred else 2, BASES * rows, GROUP * rows), BF16),
            pltpu.VMEM((patches if deferred else 1, BASES * rows, cols), F32),
            pltpu.VMEM((8 if deferred else BASES * rows, LANES if deferred else cols), BF16),
            pltpu.VMEM(((patches * rows // 8 + 2) * blocks, 8, LANES), F32),
            pltpu.SemaphoreType.DMA((groups,)),
            pltpu.SMEM((count,), I32),
            pltpu.VMEM((count,), BF16),
            pltpu.SMEM(offsets.shape, I32),
            pltpu.SMEM(coefs.shape, I32),
            *(pltpu.VMEM(m.shape, m.dtype) for m in mats),
            pltpu.SemaphoreType.DMA((5 + len(mats),)),
            pltpu.VMEM((count,), F32),
            pltpu.SemaphoreType.DMA(()),
            pltpu.SMEM((count,), F32),
            pltpu.VMEM((count,), I32),
            pltpu.SMEM((count,), I32),
            pltpu.SMEM((patches,), I32),
        ],
        cost_estimate=pl.CostEstimate(
            flops=2 * count * rows * cols * 4 * WIDE, bytes_accessed=count * rows * cols, transcendentals=0
        ),
        compiler_params=pltpu.CompilerParams(vmem_limit_bytes=48 << 20),
        name="stacks",
    )(*(pltpu.with_memory_space_constraint(a, pltpu.HBM) for a in (tile_patch, weights, offsets, coefs, tiles, *mats)))


def add_kernel(keep, got, *outs):
    start = 0
    for out in outs:
        at = slice(start, start + out.shape[0])
        out[...] = (keep[at] + got[at].astype(F32)).astype(BF16)
        start += out.shape[0]


def merge_kernel(bits, *refs):
    mine = refs[-1]
    near, cols = mine.shape
    blocks = cols // LANES
    total = refs[0][...]
    for got in refs[1:-1]:
        total = total + got[...].astype(F32)
    lane = lax.broadcasted_iota(I32, (8, LANES), 1)
    live = lane * bits < WEIGHT_BITS + 30
    value = jnp.where(live, 2.0**WEIGHT_BITS / power_of_two((lane + 1) * bits), 0.0)
    weight = jnp.sum(total[-1] * value, axis=1, keepdims=True)
    scale = jnp.where(weight > 0.0, 1.0 / jnp.sqrt(jnp.where(weight > 0.0, weight, 1.0)), 0.0)
    inner, outer = scale[0:1], scale[1:2]
    upper = lax.axis_index("visit") == 0
    for i in range(near // 8):
        here = inner
        if i == 0:
            here = jnp.where(upper, outer, inner)
        elif i == near // 8 - 1:
            here = jnp.where(upper, inner, outer)
        for b in range(blocks):
            mine[8 * i : 8 * i + 8, b * LANES : (b + 1) * LANES] = total[i * blocks + b] * here


def smooth_kernel(rows_mat, cols_mat, mine, other, coadd, detection, coadd_held, detection_held, sems):
    near, cols = mine.shape
    rows = coadd.shape[0]
    upper = lax.axis_index("visit") == 0
    top = jnp.where(upper, mine[...], other[...])
    bottom = jnp.where(upper, other[...], mine[...])
    coadd_held[: near - HALO, :] = top[HALO:]
    coadd_held[near - HALO :, :] = bottom[: near - HALO]
    moves = [pltpu.make_async_copy(coadd_held, coadd, sems.at[0])]
    moves[0].start()
    extended = jnp.concatenate([top, bottom], axis=0).astype(BF16)
    blurred = jnp.dot(rows_mat[...], extended, preferred_element_type=F32).astype(BF16)
    blocks = cols // LANES
    window = windows([block(blurred, b) for b in range(blocks)])
    parts = 2
    share = blocks // parts
    for i in range(parts):
        result = jnp.dot(
            window[i * share * rows : (i + 1) * share * rows], cols_mat[...], preferred_element_type=F32
        )
        for b in range(share):
            at = (i * share + b) * LANES
            detection_held[:, at : at + LANES] = result[b * rows : (b + 1) * rows]
        at = pl.ds(i * share * LANES, share * LANES)
        moves.append(pltpu.make_async_copy(detection_held.at[:, at], detection.at[:, at], sems.at[1 + i]))
        moves[-1].start()
    for move in moves:
        move.wait()


def shards(visit_tiles, tile_patch, offsets, psf_coefs, weights):
    rows, cols = visit_tiles.shape[1:]
    owners = lax.axis_size("patch")
    near = (rows + 2 * HALO) // 2
    bits = digit_bits(owners * lax.axis_size("visit"))
    mats = [jnp.asarray(m) for m in (lanczos_lines(), row_filters(rows), *psf_col_filters())]
    first_send, rest_send, first_keep, rest_keep = local_stacks(
        owners, bits, tile_patch, weights, offsets.T, psf_coefs.T, visit_tiles, mats
    )
    swap = [(0, 1), (1, 0)]
    beside = [(i, i ^ 1) for i in range(owners)]
    pairs = owners // 2
    cut = pairs // 2
    bounds = sorted({0, cut // 2, cut, pairs})
    first_got = lax.ppermute(first_send, "visit", swap)
    first_sums = pl.pallas_call(
        add_kernel,
        out_shape=tuple(
            jax.ShapeDtypeStruct((high - low, *first_keep.shape[1:]), BF16)
            for low, high in zip(bounds[:-2], bounds[1:-1], strict=True)
        ),
        compiler_params=pltpu.CompilerParams(vmem_limit_bytes=16 << 20),
        name="add",
    )(first_keep, first_got)
    rest = rest_keep + lax.ppermute(rest_send, "visit", swap).astype(F32)
    evens = rest[pairs - cut :]
    parts = [evens[cut]]
    for c, (low, high) in enumerate(zip(bounds[:-1], bounds[1:], strict=True)):
        crossing = first_sums[c] if high <= cut else rest[low - cut : high - cut].astype(BF16)
        crossed = lax.ppermute(crossing, "patch", beside)
        local = evens[low:high] if c == 0 else lax.optimization_barrier(evens[low:high])
        for i in range(low, high):
            e = (i + cut) % pairs
            if e == 0:
                parts.append(crossed[i - low])
            else:
                hop = [(j, j ^ (2 * e)) for j in range(owners)]
                summed = (local[i - low] + crossed[i - low].astype(F32)).astype(BF16)
                parts.append(lax.ppermute(summed, "patch", hop))
    mine = pl.pallas_call(
        functools.partial(merge_kernel, bits),
        out_shape=jax.ShapeDtypeStruct((near, cols), F32),
        compiler_params=pltpu.CompilerParams(vmem_limit_bytes=16 << 20),
        name="merge",
    )(*parts)
    other = lax.ppermute(mine, "visit", swap)
    sigma = HALO / 4.0
    out_index = np.arange(rows, dtype=np.float64)[:, None]
    in_index = np.arange(rows + 2 * HALO, dtype=np.float64)[None, :]
    rows_mat = to_bf16(gaussian(out_index + HALO - in_index, sigma, HALO))
    return pl.pallas_call(
        smooth_kernel,
        out_shape=(jax.ShapeDtypeStruct((rows, cols), F32),) * 2,
        out_specs=(pl.BlockSpec(memory_space=pltpu.HBM),) * 2,
        scratch_shapes=[
            pltpu.VMEM((rows, cols), F32),
            pltpu.VMEM((rows, cols), F32),
            pltpu.SemaphoreType.DMA((3,)),
        ],
        compiler_params=pltpu.CompilerParams(vmem_limit_bytes=8 << 20),
        name="smooth",
    )(jnp.asarray(rows_mat), jnp.asarray(col_filter(sigma, HALO)), mine, other)


def solution(mesh):
    placed = (
        P(("groups", "patch", "visit"), None, None),
        P(("groups", "patch", "visit")),
        P(("groups", "patch", "visit"), None),
        P(("groups", "patch", "visit"), None),
        P(("groups", "patch", "visit")),
    )

    return jax.shard_map(
        shards,
        mesh=mesh,
        in_specs=placed,
        out_specs=(P(("groups", "patch"), None), P(("groups", "patch"), None)),
        check_vma=False,
    )
```
